128 devices in a mesh: row: 8 (over x_lo, y), col: 16 (over z, x_hi, core).
Axes of the slice: x: 4 (x_hi: 2, x_lo: 2; x = x_hi * 2 + x_lo), y: 4, z: 4, core: 2. Of those that a mesh axis runs over, the one named last changes fastest.
Arguments:
- features: bfloat16 [65536, 256], P(('col', 'row')), may hold values from -6 to 6
- weight: bfloat16 [256, 256], replicated, may hold values from -0.375 to 0.375
- tile_values: bfloat16 [65536, 128, 128], P(('row', 'col')), may hold values from -0.046875 to 0.046875
- tile_row: int32 [65536], P(('row', 'col')), may hold values from 0 to 63, as said below
- tile_col: int32 [65536], P(('row', 'col')), may hold values from 0 to 31, as said below
- tile_count: int32 [8, 16], P('row', 'col'), may hold values from 128 to 512, as said below
- cotangent: bfloat16 [65536, 256], P(('row', 'col')), may hold values from -6 to 6
Outputs:
- activated: bfloat16 [65536, 256], P(('row', 'col'))
- grad_features: bfloat16 [65536, 256], P(('col', 'row'))
- grad_weight: float32 [256, 256], replicated
The draws below stay inside these ranges and needn't reach their ends.
Inputs may be any that keep to these rules, and one draw needn't show every extreme that they name: `tile_count`: 512 on at least one device in every draw. Within each device's slots the pairs (tile_row, tile_col) are distinct. Within each device's slots the pairs (tile_row, tile_col) are distinct.
All inputs are finite; a program needn't handle non-finite values.
Results may differ from the reference program's by a relative error of at most 0.024.
Values may be sent and summed in bfloat16 or wider, within the bound.
A program may use at most 128 MiB of HBM per device.

```python
import jax
import jax.numpy as jnp
from jax import lax

F = 256
TILE = 128
ND = 512
TMAX = 512
NODES = 65536
SLOTS = 65536
N_ROW = 8
N_COL = 16


def tile_places(key):
    row_tiles = ND * N_COL // TILE
    col_tiles = ND * N_ROW // TILE
    device_keys = jax.random.split(jax.random.fold_in(key, 11), N_ROW * N_COL)
    chosen = jax.vmap(lambda subkey: jax.random.permutation(subkey, row_tiles * col_tiles)[:TMAX])(device_keys)
    return (chosen.reshape(-1).astype(jnp.int32), col_tiles)


def draw_tile_row(key, part):
    chosen, col_tiles = tile_places(key)
    return (chosen // col_tiles).astype(jnp.int32)


def draw_tile_col(key, part):
    chosen, col_tiles = tile_places(key)
    return (chosen % col_tiles).astype(jnp.int32)


def draw_tile_count(key, part):
    first_key, second_key = jax.random.split(jax.random.fold_in(key, 5))
    counts = jax.random.randint(first_key, (N_ROW * N_COL,), TMAX // 4, TMAX + 1)
    busiest = jax.random.randint(second_key, (), 0, N_ROW * N_COL)
    counts = jnp.where(jnp.arange(N_ROW * N_COL) == busiest, TMAX, counts)
    return counts.reshape(N_ROW, N_COL).astype(jnp.int32)


def block_levels(key, shape, cuts, smallest, top_value):
    def one(axis_at, blocks):
        draws = jax.random.uniform(jax.random.fold_in(jax.random.fold_in(key, 6), axis_at), (blocks,), jnp.float32, smallest / len(cuts), top_value / len(cuts))
        return jnp.repeat(jnp.exp(draws), shape[axis_at] // blocks).reshape((-1,) + (1,) * (len(shape) - axis_at - 1))

    level = one(*cuts[0])
    for cut in cuts[1:]:
        level = level * one(*cut)
    return level


def gaussian(rng, shape, spread, reach, cuts=(), held_as=jnp.bfloat16):
    drawn = jax.random.normal(rng, shape, jnp.float32) * spread
    if len(cuts) > 0:
        drawn = block_levels(rng, shape, cuts, -0.22, 0.18) * drawn
    return jnp.clip(drawn, min=-reach, max=reach).astype(held_as)


def setup_inputs(seed: int = 0) -> dict:
    keys = jax.random.split(jax.random.key(seed), 8)
    return {
        "features": gaussian(keys[0], (NODES, F), 1.0, 6.0, ((0, 128),)),
        "weight": gaussian(keys[1], (F, F), F ** -0.5, 0.375),
        "tile_values": gaussian(keys[2], (SLOTS, TILE, TILE), (TMAX * TILE * TILE // ND) ** -0.5, 0.046875, ((0, 128),)),
        "tile_row": draw_tile_row(jax.random.fold_in(keys[7], 71), 0),
        "tile_col": draw_tile_col(jax.random.fold_in(keys[7], 71), 0),
        "tile_count": draw_tile_count(jax.random.fold_in(keys[7], 71), 0),
        "cotangent": gaussian(keys[6], (NODES, F), 1.0, 6.0, ((0, 128),)),
    }


def silu_slope(values):
    sigma = jax.nn.sigmoid(values)
    return sigma * (1.0 + values * (1.0 - sigma))


def round_keep(values):
    return lax.optimization_barrier(values.astype(jnp.bfloat16)).astype(jnp.float32)


def reference(features, weight, tile_values, tile_row, tile_col, tile_count, cotangent):
    row_tiles = ND * N_COL // TILE
    col_tiles = ND * N_ROW // TILE
    projected = jnp.dot(features, weight, preferred_element_type=jnp.float32).astype(jnp.bfloat16)
    panel_grid = projected.reshape(N_COL, col_tiles, TILE, F)
    tile_grid = tile_values.reshape(N_ROW, N_COL, TMAX, TILE, TILE)
    row_grid = tile_row.reshape(N_ROW, N_COL, TMAX)
    col_grid = tile_col.reshape(N_ROW, N_COL, TMAX)
    live_grid = (jnp.arange(TMAX, dtype=jnp.int32)[None, None, :] < tile_count[:, :, None]).astype(jnp.float32)

    def forward_term(row_id, col_id):
        blocks = tile_grid[row_id, col_id].astype(jnp.float32)
        fetched = panel_grid[col_id][col_grid[row_id, col_id]].astype(jnp.float32)
        product = jnp.einsum("sab,sbf->saf", blocks, fetched) * live_grid[row_id, col_id][:, None, None]
        part = jnp.zeros((row_tiles, TILE, F), jnp.float32).at[row_grid[row_id, col_id]].add(product)
        return round_keep(part.reshape(row_tiles * TILE, F))

    def row_total(row_id):
        def step(running, col_id):
            return running + forward_term(row_id, col_id), None
        start_value = jnp.zeros((row_tiles * TILE, F), jnp.float32)
        return lax.scan(step, start_value, jnp.arange(N_COL, dtype=jnp.int32))[0]

    summed = lax.map(row_total, jnp.arange(N_ROW, dtype=jnp.int32)).reshape(NODES, F)
    activated = jax.nn.silu(summed).astype(jnp.bfloat16)
    slope = (cotangent.astype(jnp.float32) * silu_slope(summed)).astype(jnp.bfloat16)
    slope_grid = slope.reshape(N_ROW, row_tiles, TILE, F)

    def backward_term(row_id, col_id):
        blocks = tile_grid[row_id, col_id].astype(jnp.float32)
        fetched = slope_grid[row_id][row_grid[row_id, col_id]].astype(jnp.float32)
        product = jnp.einsum("sab,saf->sbf", blocks, fetched) * live_grid[row_id, col_id][:, None, None]
        part = jnp.zeros((col_tiles, TILE, F), jnp.float32).at[col_grid[row_id, col_id]].add(product)
        return round_keep(part.reshape(col_tiles * TILE, F))

    def col_total(col_id):
        def step(running, row_id):
            return running + backward_term(row_id, col_id), None
        start_value = jnp.zeros((col_tiles * TILE, F), jnp.float32)
        return lax.scan(step, start_value, jnp.arange(N_ROW, dtype=jnp.int32))[0]

    grad_nodes = lax.map(col_total, jnp.arange(N_COL, dtype=jnp.int32)).reshape(NODES, F).astype(jnp.bfloat16)
    grad_features = jnp.dot(grad_nodes, weight.T, preferred_element_type=jnp.float32).astype(jnp.bfloat16)
    grad_weight = jnp.dot(features.T, grad_nodes, preferred_element_type=jnp.float32)
    return (activated, grad_features, grad_weight)
```

```python
import functools

import jax
import jax.numpy as jnp
from jax import lax
from jax.experimental import pallas as pl
from jax.experimental.pallas import tpu as pltpu
from jax.sharding import PartitionSpec as P


GROUP = 32
CHUNK = 256


def silu_slope(values):
    sigma = jax.nn.sigmoid(values)
    return sigma * (1.0 + values * (1.0 - sigma))


def tile_kernel(count_ref, place_ref, fetch_ref, tiles_ref, src_ref, out_ref, acc_ref, *, forward):
    step = pl.program_id(0)
    tile = tiles_ref.shape[1]
    group = tiles_ref.shape[0]
    out_rows = acc_ref.shape[0]

    @pl.when(step == 0)
    def _():
        def zero(k, carry):
            rows = pl.ds(pl.multiple_of(k * CHUNK, CHUNK), CHUNK)
            acc_ref[rows, :] = jnp.zeros((CHUNK, acc_ref.shape[1]), jnp.float32)
            return carry

        lax.fori_loop(0, out_rows // CHUNK, zero, 0)

    base = step * group
    live = jnp.clip(count_ref[0] - base, 0, group)

    def body(j, carry):
        slot = base + j
        src_rows = pl.ds(pl.multiple_of(fetch_ref[slot] * tile, tile), tile)
        dst_rows = pl.ds(pl.multiple_of(place_ref[slot] * tile, tile), tile)
        block = tiles_ref[j]
        src = src_ref[src_rows, :]
        if forward:
            prod = jnp.dot(block, src, preferred_element_type=jnp.float32)
        else:
            prod = lax.dot_general(
                block, src, (((0,), (0,)), ((), ())), preferred_element_type=jnp.float32
            )
        acc_ref[dst_rows, :] += prod
        return carry

    lax.fori_loop(0, live, body, 0)

    @pl.when(step == pl.num_programs(0) - 1)
    def _():
        def emit(k, carry):
            rows = pl.ds(pl.multiple_of(k * CHUNK, CHUNK), CHUNK)
            out_ref[rows, :] = acc_ref[rows, :].astype(out_ref.dtype)
            return carry

        lax.fori_loop(0, out_rows // CHUNK, emit, 0)


def tile_products(tile_values, fetch_index, place_index, count, source, out_tiles, forward):
    slots, tile, _ = tile_values.shape
    hidden = source.shape[-1]
    src_rows = source.shape[0]
    out_rows = out_tiles * tile
    group = GROUP
    steps = slots // group

    def tiles_map(i, count_ref, place_ref, fetch_ref):
        last = jnp.maximum(count_ref[0] - 1, 0) // group
        return (jnp.minimum(i, last), 0, 0)

    grid_spec = pltpu.PrefetchScalarGridSpec(
        num_scalar_prefetch=3,
        grid=(steps,),
        in_specs=[
            pl.BlockSpec((group, tile, tile), tiles_map),
            pl.BlockSpec((src_rows, hidden), lambda i, *_: (0, 0)),
        ],
        out_specs=pl.BlockSpec((out_rows, hidden), lambda i, *_: (0, 0)),
        scratch_shapes=[pltpu.VMEM((out_rows, hidden), jnp.float32)],
    )
    flops = 2 * slots * tile * tile * hidden
    return pl.pallas_call(
        functools.partial(tile_kernel, forward=forward),
        grid_spec=grid_spec,
        out_shape=jax.ShapeDtypeStruct((out_rows, hidden), jnp.bfloat16),
        compiler_params=pltpu.CompilerParams(
            dimension_semantics=("arbitrary",), vmem_limit_bytes=48 * 1024 * 1024
        ),
        cost_estimate=pl.CostEstimate(
            flops=flops,
            bytes_accessed=slots * tile * tile * 2 + src_rows * hidden * 2 + out_rows * hidden * 2,
            transcendentals=0,
        ),
    )(count, place_index, fetch_index, tile_values, source)


def body(features, weight, tile_values, tile_row, tile_col, tile_count, cotangent):
    row_count = lax.axis_size("row")
    col_count = lax.axis_size("col")
    node_dev = features.shape[0]
    tile_size = tile_values.shape[1]
    row_tiles = node_dev * col_count // tile_size
    col_tiles = node_dev * row_count // tile_size
    count = tile_count.reshape(1)
    projected = jnp.dot(features, weight, preferred_element_type=jnp.float32).astype(jnp.bfloat16)
    panel_rows = lax.all_gather(projected, "row", axis=0, tiled=True)
    forward_part = tile_products(
        tile_values, tile_col, tile_row, count, panel_rows, row_tiles, True
    )
    summed = lax.psum_scatter(forward_part, "col", scatter_dimension=0, tiled=True).astype(
        jnp.float32
    )
    activated = jax.nn.silu(summed).astype(jnp.bfloat16)
    slope = (cotangent.astype(jnp.float32) * silu_slope(summed)).astype(jnp.bfloat16)
    slope_full = lax.all_gather(slope, "col", axis=0, tiled=True)
    column_part = tile_products(
        tile_values, tile_row, tile_col, count, slope_full, col_tiles, False
    )
    grad_nodes = (
        lax.psum_scatter(column_part, "row", scatter_dimension=0, tiled=True)
        .astype(jnp.float32)
        .astype(jnp.bfloat16)
    )
    grad_features = lax.dot_general(
        grad_nodes, weight, (((1,), (1,)), ((), ())), preferred_element_type=jnp.float32
    ).astype(jnp.bfloat16)
    weight_term = lax.dot_general(
        features, grad_nodes, (((0,), (0,)), ((), ())), preferred_element_type=jnp.float32
    )
    grad_weight = lax.psum(weight_term, ("row", "col"))
    return (activated, grad_features, grad_weight)


def solution(mesh):
    placed = (
        P(("col", "row"), None),
        P(),
        P(("row", "col"), None, None),
        P(("row", "col")),
        P(("row", "col")),
        P("row", "col"),
        P(("row", "col"), None),
    )
    return jax.shard_map(
        body,
        mesh=mesh,
        in_specs=placed,
        out_specs=(P(("row", "col"), None), P(("col", "row"), None), P()),
        check_vma=False,
    )
```

```python
import functools

import jax
import jax.numpy as jnp
from jax import lax
from jax.experimental import pallas as pl
from jax.experimental.pallas import tpu as pltpu
from jax.sharding import PartitionSpec as P


GROUP = 32
CHUNK = 256
UNROLL = 4


def silu_slope(values):
    sigma = jax.nn.sigmoid(values)
    return sigma * (1.0 + values * (1.0 - sigma))


def tile_kernel(count_ref, place_ref, fetch_ref, tiles_ref, src_ref, out_ref, acc_ref, *, forward):
    step = pl.program_id(0)
    tile = tiles_ref.shape[1]
    group = tiles_ref.shape[0]
    out_rows = acc_ref.shape[0]

    @pl.when(step == 0)
    def _():
        def zero(k, carry):
            rows = pl.ds(pl.multiple_of(k * CHUNK, CHUNK), CHUNK)
            acc_ref[rows, :] = jnp.zeros((CHUNK, acc_ref.shape[1]), jnp.float32)
            return carry

        lax.fori_loop(0, out_rows // CHUNK, zero, 0)

    base = step * group
    live = jnp.clip(count_ref[0] - base, 0, group)

    def product(slot, j):
        src_rows = pl.ds(pl.multiple_of(fetch_ref[slot] * tile, tile), tile)
        block = tiles_ref[j]
        src = src_ref[src_rows, :]
        if forward:
            return jnp.dot(block, src, preferred_element_type=jnp.float32)
        return lax.dot_general(
            block, src, (((0,), (0,)), ((), ())), preferred_element_type=jnp.float32
        )

    def add(slot, prod):
        dst_rows = pl.ds(pl.multiple_of(place_ref[slot] * tile, tile), tile)
        acc_ref[dst_rows, :] += prod

    def many(k, carry):
        j0 = k * UNROLL
        prods = [product(base + j0 + u, j0 + u) for u in range(UNROLL)]
        for u in range(UNROLL):
            add(base + j0 + u, prods[u])
        return carry

    def one(j, carry):
        add(base + j, product(base + j, j))
        return carry

    full = live // UNROLL
    lax.fori_loop(0, full, many, 0)
    lax.fori_loop(full * UNROLL, live, one, 0)

    @pl.when(step == pl.num_programs(0) - 1)
    def _():
        def emit(k, carry):
            rows = pl.ds(pl.multiple_of(k * CHUNK, CHUNK), CHUNK)
            out_ref[rows, :] = acc_ref[rows, :].astype(out_ref.dtype)
            return carry

        lax.fori_loop(0, out_rows // CHUNK, emit, 0)


def tile_products(tile_values, fetch_index, place_index, count, source, out_tiles, forward):
    slots, tile, _ = tile_values.shape
    hidden = source.shape[-1]
    src_rows = source.shape[0]
    out_rows = out_tiles * tile
    group = GROUP
    steps = slots // group

    def tiles_map(i, count_ref, place_ref, fetch_ref):
        last = jnp.maximum(count_ref[0] - 1, 0) // group
        return (jnp.minimum(i, last), 0, 0)

    grid_spec = pltpu.PrefetchScalarGridSpec(
        num_scalar_prefetch=3,
        grid=(steps,),
        in_specs=[
            pl.BlockSpec((group, tile, tile), tiles_map),
            pl.BlockSpec((src_rows, hidden), lambda i, *_: (0, 0)),
        ],
        out_specs=pl.BlockSpec((out_rows, hidden), lambda i, *_: (0, 0)),
        scratch_shapes=[pltpu.VMEM((out_rows, hidden), jnp.float32)],
    )
    flops = 2 * slots * tile * tile * hidden
    return pl.pallas_call(
        functools.partial(tile_kernel, forward=forward),
        grid_spec=grid_spec,
        out_shape=jax.ShapeDtypeStruct((out_rows, hidden), jnp.bfloat16),
        compiler_params=pltpu.CompilerParams(
            dimension_semantics=("arbitrary",), vmem_limit_bytes=48 * 1024 * 1024
        ),
        cost_estimate=pl.CostEstimate(
            flops=flops,
            bytes_accessed=slots * tile * tile * 2 + src_rows * hidden * 2 + out_rows * hidden * 2,
            transcendentals=0,
        ),
    )(count, place_index, fetch_index, tile_values, source)


def body(features, weight, tile_values, tile_row, tile_col, tile_count, cotangent):
    row_count = lax.axis_size("row")
    col_count = lax.axis_size("col")
    node_dev = features.shape[0]
    tile_size = tile_values.shape[1]
    row_tiles = node_dev * col_count // tile_size
    col_tiles = node_dev * row_count // tile_size
    count = tile_count.reshape(1)
    projected = jnp.dot(features, weight, preferred_element_type=jnp.float32).astype(jnp.bfloat16)
    panel_rows = lax.all_gather(projected, "row", axis=0, tiled=True)
    forward_part = tile_products(
        tile_values, tile_col, tile_row, count, panel_rows, row_tiles, True
    )
    summed = lax.psum_scatter(forward_part, "col", scatter_dimension=0, tiled=True).astype(
        jnp.float32
    )
    activated = jax.nn.silu(summed).astype(jnp.bfloat16)
    slope = (cotangent.astype(jnp.float32) * silu_slope(summed)).astype(jnp.bfloat16)
    slope_full = lax.all_gather(slope, "col", axis=0, tiled=True)
    column_part = tile_products(
        tile_values, tile_row, tile_col, count, slope_full, col_tiles, False
    )
    grad_nodes = (
        lax.psum_scatter(column_part, "row", scatter_dimension=0, tiled=True)
        .astype(jnp.float32)
        .astype(jnp.bfloat16)
    )
    grad_features = lax.dot_general(
        grad_nodes, weight, (((1,), (1,)), ((), ())), preferred_element_type=jnp.float32
    ).astype(jnp.bfloat16)
    weight_term = lax.dot_general(
        features, grad_nodes, (((0,), (0,)), ((), ())), preferred_element_type=jnp.float32
    )
    grad_weight = lax.psum(weight_term, ("row", "col"))
    return (activated, grad_features, grad_weight)


def solution(mesh):
    placed = (
        P(("col", "row"), None),
        P(),
        P(("row", "col"), None, None),
        P(("row", "col")),
        P(("row", "col")),
        P("row", "col"),
        P(("row", "col"), None),
    )
    return jax.shard_map(
        body,
        mesh=mesh,
        in_specs=placed,
        out_specs=(P(("row", "col"), None), P(("col", "row"), None), P()),
        check_vma=False,
    )
```

```python
import functools

import jax
import jax.numpy as jnp
from jax import lax
from jax.experimental import pallas as pl
from jax.experimental.pallas import tpu as pltpu
from jax.sharding import PartitionSpec as P


GROUP = 32
CHUNK = 256
UNROLL = 4


def silu_slope(values):
    sigma = jax.nn.sigmoid(values)
    return sigma * (1.0 + values * (1.0 - sigma))


def tile_kernel(count_ref, place_ref, fetch_ref, tiles_ref, src_ref, out_ref, acc_ref, *, forward):
    step = pl.program_id(0)
    tile = tiles_ref.shape[1]
    group = tiles_ref.shape[0]
    out_rows = acc_ref.shape[0]

    @pl.when(step == 0)
    def _():
        def zero(k, carry):
            rows = pl.ds(pl.multiple_of(k * CHUNK, CHUNK), CHUNK)
            acc_ref[rows, :] = jnp.zeros((CHUNK, acc_ref.shape[1]), jnp.float32)
            return carry

        lax.fori_loop(0, out_rows // CHUNK, zero, 0)

    base = step * group
    live = jnp.clip(count_ref[0] - base, 0, group)

    def product(slot, j):
        src_rows = pl.ds(pl.multiple_of(fetch_ref[slot] * tile, tile), tile)
        block = tiles_ref[j]
        src = src_ref[src_rows, :]
        if forward:
            return jnp.dot(block, src, preferred_element_type=jnp.float32)
        return lax.dot_general(
            block, src, (((0,), (0,)), ((), ())), preferred_element_type=jnp.float32
        )

    def add(slot, prod):
        dst_rows = pl.ds(pl.multiple_of(place_ref[slot] * tile, tile), tile)
        acc_ref[dst_rows, :] += prod

    def many(k, carry):
        j0 = k * UNROLL
        prods = [product(base + j0 + u, j0 + u) for u in range(UNROLL)]
        for u in range(UNROLL):
            add(base + j0 + u, prods[u])
        return carry

    def one(j, carry):
        add(base + j, product(base + j, j))
        return carry

    full = live // UNROLL
    lax.fori_loop(0, full, many, 0)
    lax.fori_loop(full * UNROLL, live, one, 0)

    @pl.when(step == pl.num_programs(0) - 1)
    def _():
        def emit(k, carry):
            rows = pl.ds(pl.multiple_of(k * CHUNK, CHUNK), CHUNK)
            out_ref[rows, :] = acc_ref[rows, :].astype(out_ref.dtype)
            return carry

        lax.fori_loop(0, out_rows // CHUNK, emit, 0)


def tile_products(tile_values, fetch_index, place_index, count, source, out_tiles, forward):
    slots, tile, _ = tile_values.shape
    hidden = source.shape[-1]
    src_rows = source.shape[0]
    out_rows = out_tiles * tile
    group = GROUP
    steps = slots // group

    def tiles_map(i, count_ref, place_ref, fetch_ref):
        last = jnp.maximum(count_ref[0] - 1, 0) // group
        return (jnp.minimum(i, last), 0, 0)

    grid_spec = pltpu.PrefetchScalarGridSpec(
        num_scalar_prefetch=3,
        grid=(steps,),
        in_specs=[
            pl.BlockSpec((group, tile, tile), tiles_map),
            pl.BlockSpec((src_rows, hidden), lambda i, *_: (0, 0)),
        ],
        out_specs=pl.BlockSpec((out_rows, hidden), lambda i, *_: (0, 0)),
        scratch_shapes=[pltpu.VMEM((out_rows, hidden), jnp.float32)],
    )
    flops = 2 * slots * tile * tile * hidden
    return pl.pallas_call(
        functools.partial(tile_kernel, forward=forward),
        grid_spec=grid_spec,
        out_shape=jax.ShapeDtypeStruct((out_rows, hidden), jnp.bfloat16),
        compiler_params=pltpu.CompilerParams(
            dimension_semantics=("arbitrary",), vmem_limit_bytes=48 * 1024 * 1024
        ),
        cost_estimate=pl.CostEstimate(
            flops=flops,
            bytes_accessed=slots * tile * tile * 2 + src_rows * hidden * 2 + out_rows * hidden * 2,
            transcendentals=0,
        ),
    )(count, place_index, fetch_index, tile_values, source)


def gather_rows(values, axes, parts):
    copies = jnp.broadcast_to(values[None], (parts,) + values.shape)
    return lax.all_to_all(copies, axes, 0, 0, tiled=True).reshape(-1, values.shape[-1])


def scatter_sum(values, axes, parts):
    pieces = lax.all_to_all(values.reshape(parts, -1, values.shape[-1]), axes, 0, 0, tiled=False)
    return pieces.astype(jnp.float32).sum(0)


def body(features, weight, tile_values, tile_row, tile_col, tile_count, cotangent):
    row_count = lax.axis_size("row")
    col_count = lax.axis_size("col")
    node_dev = features.shape[0]
    tile_size = tile_values.shape[1]
    row_tiles = node_dev * col_count // tile_size
    col_tiles = node_dev * row_count // tile_size
    count = tile_count.reshape(1)
    projected = jnp.dot(features, weight, preferred_element_type=jnp.float32).astype(jnp.bfloat16)
    panel_rows = gather_rows(projected, "row", row_count)
    forward_part = tile_products(
        tile_values, tile_col, tile_row, count, panel_rows, row_tiles, True
    )
    summed = scatter_sum(forward_part, "col", col_count)
    activated = jax.nn.silu(summed).astype(jnp.bfloat16)
    slope = (cotangent.astype(jnp.float32) * silu_slope(summed)).astype(jnp.bfloat16)
    slope_full = gather_rows(slope, "col", col_count)
    column_part = tile_products(
        tile_values, tile_row, tile_col, count, slope_full, col_tiles, False
    )
    grad_nodes = scatter_sum(column_part, "row", row_count).astype(jnp.bfloat16)
    grad_features = lax.dot_general(
        grad_nodes, weight, (((1,), (1,)), ((), ())), preferred_element_type=jnp.float32
    ).astype(jnp.bfloat16)
    weight_term = lax.dot_general(
        features, grad_nodes, (((0,), (0,)), ((), ())), preferred_element_type=jnp.float32
    )
    devices = row_count * col_count
    weight_piece = scatter_sum(weight_term, ("row", "col"), devices)
    grad_weight = gather_rows(weight_piece, ("row", "col"), devices)
    return (activated, grad_features, grad_weight)


def solution(mesh):
    placed = (
        P(("col", "row"), None),
        P(),
        P(("row", "col"), None, None),
        P(("row", "col")),
        P(("row", "col")),
        P("row", "col"),
        P(("row", "col"), None),
    )
    return jax.shard_map(
        body,
        mesh=mesh,
        in_specs=placed,
        out_specs=(P(("row", "col"), None), P(("col", "row"), None), P()),
        check_vma=False,
    )
```

```python
import functools

import jax
import jax.numpy as jnp
from jax import lax
from jax.experimental import pallas as pl
from jax.experimental.pallas import tpu as pltpu
from jax.sharding import PartitionSpec as P


GROUP = 32
CHUNK = 256
UNROLL = 4
SPLIT = 2


def silu_slope(values):
    sigma = jax.nn.sigmoid(values)
    return sigma * (1.0 + values * (1.0 - sigma))


def tile_kernel(count_ref, place_ref, fetch_ref, tiles_ref, src_ref, out_ref, acc_ref, *, forward):
    step = pl.program_id(0)
    tile = tiles_ref.shape[1]
    group = tiles_ref.shape[0]
    out_rows = acc_ref.shape[0]

    @pl.when(step == 0)
    def _():
        def zero(k, carry):
            rows = pl.ds(pl.multiple_of(k * CHUNK, CHUNK), CHUNK)
            acc_ref[rows, :] = jnp.zeros((CHUNK, acc_ref.shape[1]), jnp.float32)
            return carry

        lax.fori_loop(0, out_rows // CHUNK, zero, 0)

    base = step * group
    live = jnp.clip(count_ref[0] - base, 0, group)

    def product(slot, j):
        src_rows = pl.ds(pl.multiple_of(fetch_ref[slot] * tile, tile), tile)
        block = tiles_ref[j]
        src = src_ref[src_rows, :]
        if forward:
            return jnp.dot(block, src, preferred_element_type=jnp.float32)
        return lax.dot_general(
            block, src, (((0,), (0,)), ((), ())), preferred_element_type=jnp.float32
        )

    def add(slot, prod):
        dst_rows = pl.ds(pl.multiple_of(place_ref[slot] * tile, tile), tile)
        acc_ref[dst_rows, :] += prod

    def many(k, carry):
        j0 = k * UNROLL
        prods = [product(base + j0 + u, j0 + u) for u in range(UNROLL)]
        for u in range(UNROLL):
            add(base + j0 + u, prods[u])
        return carry

    def one(j, carry):
        add(base + j, product(base + j, j))
        return carry

    full = live // UNROLL
    lax.fori_loop(0, full, many, 0)
    lax.fori_loop(full * UNROLL, live, one, 0)

    @pl.when(step == pl.num_programs(0) - 1)
    def _():
        def emit(k, carry):
            rows = pl.ds(pl.multiple_of(k * CHUNK, CHUNK), CHUNK)
            out_ref[rows, :] = acc_ref[rows, :].astype(out_ref.dtype)
            return carry

        lax.fori_loop(0, out_rows // CHUNK, emit, 0)


def tile_products(tile_values, fetch_index, place_index, count, source, out_tiles, forward, part=0, hidden=None):
    slots, tile, _ = tile_values.shape
    hidden = source.shape[-1] if hidden is None else hidden
    src_rows = source.shape[0]
    out_rows = out_tiles * tile
    group = GROUP
    steps = slots // group

    def tiles_map(i, count_ref, place_ref, fetch_ref):
        last = jnp.maximum(count_ref[0] - 1, 0) // group
        return (jnp.minimum(i, last), 0, 0)

    grid_spec = pltpu.PrefetchScalarGridSpec(
        num_scalar_prefetch=3,
        grid=(steps,),
        in_specs=[
            pl.BlockSpec((group, tile, tile), tiles_map),
            pl.BlockSpec((src_rows, hidden), lambda i, *_: (0, part)),
        ],
        out_specs=pl.BlockSpec((out_rows, hidden), lambda i, *_: (0, 0)),
        scratch_shapes=[pltpu.VMEM((out_rows, hidden), jnp.float32)],
    )
    flops = 2 * slots * tile * tile * hidden
    return pl.pallas_call(
        functools.partial(tile_kernel, forward=forward),
        grid_spec=grid_spec,
        out_shape=jax.ShapeDtypeStruct((out_rows, hidden), jnp.bfloat16),
        compiler_params=pltpu.CompilerParams(
            dimension_semantics=("arbitrary",), vmem_limit_bytes=48 * 1024 * 1024
        ),
        cost_estimate=pl.CostEstimate(
            flops=flops,
            bytes_accessed=slots * tile * tile * 2 + src_rows * hidden * 2 + out_rows * hidden * 2,
            transcendentals=0,
        ),
    )(count, place_index, fetch_index, tile_values, source)


def gather_rows(values, axes, parts):
    copies = jnp.broadcast_to(values[None], (parts,) + values.shape)
    return lax.all_to_all(copies, axes, 0, 0, tiled=True).reshape(-1, values.shape[-1])


def scatter_sum(values, axes, parts):
    pieces = lax.all_to_all(values.reshape(parts, -1, values.shape[-1]), axes, 0, 0, tiled=False)
    return pieces.astype(jnp.float32).sum(0)


def body(features, weight, tile_values, tile_row, tile_col, tile_count, cotangent):
    row_count = lax.axis_size("row")
    col_count = lax.axis_size("col")
    node_dev = features.shape[0]
    hidden = features.shape[1]
    tile_size = tile_values.shape[1]
    row_tiles = node_dev * col_count // tile_size
    col_tiles = node_dev * row_count // tile_size
    count = tile_count.reshape(1)
    width = hidden // SPLIT
    projected = jnp.dot(features, weight, preferred_element_type=jnp.float32).astype(jnp.bfloat16)
    panel_rows = gather_rows(projected, "row", row_count)
    activated_parts = []
    grad_parts = []
    for part in range(SPLIT):
        forward_part = tile_products(
            tile_values, tile_col, tile_row, count, panel_rows, row_tiles, True, part, width
        )
        summed = scatter_sum(forward_part, "col", col_count)
        activated_parts.append(jax.nn.silu(summed).astype(jnp.bfloat16))
        cot = cotangent[:, part * width:(part + 1) * width].astype(jnp.float32)
        slope = (cot * silu_slope(summed)).astype(jnp.bfloat16)
        slope_full = gather_rows(slope, "col", col_count)
        column_part = tile_products(
            tile_values, tile_row, tile_col, count, slope_full, col_tiles, False
        )
        grad_parts.append(scatter_sum(column_part, "row", row_count))
    activated = jnp.concatenate(activated_parts, axis=1)
    grad_nodes = jnp.concatenate(grad_parts, axis=1).astype(jnp.bfloat16)
    grad_features = lax.dot_general(
        grad_nodes, weight, (((1,), (1,)), ((), ())), preferred_element_type=jnp.float32
    ).astype(jnp.bfloat16)
    weight_term = lax.dot_general(
        features, grad_nodes, (((0,), (0,)), ((), ())), preferred_element_type=jnp.float32
    )
    devices = row_count * col_count
    weight_piece = scatter_sum(weight_term, ("row", "col"), devices)
    grad_weight = gather_rows(weight_piece, ("row", "col"), devices)
    return (activated, grad_features, grad_weight)


def solution(mesh):
    placed = (
        P(("col", "row"), None),
        P(),
        P(("row", "col"), None, None),
        P(("row", "col")),
        P(("row", "col")),
        P("row", "col"),
        P(("row", "col"), None),
    )
    return jax.shard_map(
        body,
        mesh=mesh,
        in_specs=placed,
        out_specs=(P(("row", "col"), None), P(("col", "row"), None), P()),
        check_vma=False,
    )
```

```python
import functools

import jax
import jax.numpy as jnp
from jax import lax
from jax.experimental import pallas as pl
from jax.experimental.pallas import tpu as pltpu
from jax.sharding import Mesh, PartitionSpec as P


GROUP = 32
CHUNK = 256
UNROLL = 4


def silu_slope(values):
    sigma = jax.nn.sigmoid(values)
    return sigma * (1.0 + values * (1.0 - sigma))


def tile_kernel(count_ref, place_ref, fetch_ref, tiles_ref, src_ref, out_ref, acc_ref, *, forward):
    step = pl.program_id(0)
    tile = tiles_ref.shape[1]
    group = tiles_ref.shape[0]
    out_rows = acc_ref.shape[0]

    @pl.when(step == 0)
    def _():
        def zero(k, carry):
            rows = pl.ds(pl.multiple_of(k * CHUNK, CHUNK), CHUNK)
            acc_ref[rows, :] = jnp.zeros((CHUNK, acc_ref.shape[1]), jnp.float32)
            return carry

        lax.fori_loop(0, out_rows // CHUNK, zero, 0)

    base = step * group
    live = jnp.clip(count_ref[0] - base, 0, group)

    def product(slot, j):
        src_rows = pl.ds(pl.multiple_of(fetch_ref[slot] * tile, tile), tile)
        block = tiles_ref[j]
        src = src_ref[src_rows, :]
        if forward:
            return jnp.dot(block, src, preferred_element_type=jnp.float32)
        return lax.dot_general(
            block, src, (((0,), (0,)), ((), ())), preferred_element_type=jnp.float32
        )

    def add(slot, prod):
        dst_rows = pl.ds(pl.multiple_of(place_ref[slot] * tile, tile), tile)
        acc_ref[dst_rows, :] += prod

    def many(k, carry):
        j0 = k * UNROLL
        prods = [product(base + j0 + u, j0 + u) for u in range(UNROLL)]
        for u in range(UNROLL):
            add(base + j0 + u, prods[u])
        return carry

    def one(j, carry):
        add(base + j, product(base + j, j))
        return carry

    full = live // UNROLL
    lax.fori_loop(0, full, many, 0)
    lax.fori_loop(full * UNROLL, live, one, 0)

    @pl.when(step == pl.num_programs(0) - 1)
    def _():
        def emit(k, carry):
            rows = pl.ds(pl.multiple_of(k * CHUNK, CHUNK), CHUNK)
            out_ref[rows, :] = acc_ref[rows, :].astype(out_ref.dtype)
            return carry

        lax.fori_loop(0, out_rows // CHUNK, emit, 0)


def tile_products(tile_values, fetch_index, place_index, count, source, out_tiles, forward):
    slots, tile, _ = tile_values.shape
    hidden = source.shape[-1]
    src_rows = source.shape[0]
    out_rows = out_tiles * tile
    group = GROUP
    steps = slots // group

    def tiles_map(i, count_ref, place_ref, fetch_ref):
        last = jnp.maximum(count_ref[0] - 1, 0) // group
        return (jnp.minimum(i, last), 0, 0)

    grid_spec = pltpu.PrefetchScalarGridSpec(
        num_scalar_prefetch=3,
        grid=(steps,),
        in_specs=[
            pl.BlockSpec((group, tile, tile), tiles_map),
            pl.BlockSpec((src_rows, hidden), lambda i, *_: (0, 0)),
        ],
        out_specs=pl.BlockSpec((out_rows, hidden), lambda i, *_: (0, 0)),
        scratch_shapes=[pltpu.VMEM((out_rows, hidden), jnp.float32)],
    )
    flops = 2 * slots * tile * tile * hidden
    return pl.pallas_call(
        functools.partial(tile_kernel, forward=forward),
        grid_spec=grid_spec,
        out_shape=jax.ShapeDtypeStruct((out_rows, hidden), jnp.bfloat16),
        compiler_params=pltpu.CompilerParams(
            dimension_semantics=("arbitrary",), vmem_limit_bytes=48 * 1024 * 1024
        ),
        cost_estimate=pl.CostEstimate(
            flops=flops,
            bytes_accessed=slots * tile * tile * 2 + src_rows * hidden * 2 + out_rows * hidden * 2,
            transcendentals=0,
        ),
    )(count, place_index, fetch_index, tile_values, source)


def gather_rows(values, axes, parts):
    copies = jnp.broadcast_to(values[None], (parts,) + values.shape)
    return lax.all_to_all(copies, axes, 0, 0, tiled=True).reshape(-1, values.shape[-1])


def scatter_sum(values, axes, parts):
    pieces = lax.all_to_all(values.reshape(parts, -1, values.shape[-1]), axes, 0, 0, tiled=False)
    return pieces.astype(jnp.float32).sum(0)


def body(features, weight, tile_values, tile_row, tile_col, tile_count, cotangent):
    row_count = lax.axis_size("row")
    pair_count = lax.axis_size("colhi")
    core_count = lax.axis_size("core")
    col_count = pair_count * core_count
    node_dev = features.shape[0]
    hidden = features.shape[1]
    tile_size = tile_values.shape[1]
    per_dev = node_dev // tile_size
    row_tiles = node_dev * col_count // tile_size
    col_tiles = node_dev * row_count // tile_size
    count = tile_count.reshape(1)
    projected = jnp.dot(features, weight, preferred_element_type=jnp.float32).astype(jnp.bfloat16)
    panel_rows = gather_rows(projected, "row", row_count)
    forward_part = tile_products(
        tile_values, tile_col, tile_row, count, panel_rows, row_tiles, True
    )
    by_core = forward_part.reshape(pair_count, core_count, node_dev, hidden)
    on_chip = lax.all_to_all(by_core, "core", 1, 1, tiled=False)
    chip_sum = on_chip.astype(jnp.float32).sum(1).astype(jnp.bfloat16)
    summed = scatter_sum(chip_sum, "colhi", pair_count)
    activated = jax.nn.silu(summed).astype(jnp.bfloat16)
    slope = (cotangent.astype(jnp.float32) * silu_slope(summed)).astype(jnp.bfloat16)
    slope_pairs = gather_rows(slope, "colhi", pair_count)
    slope_full = gather_rows(slope_pairs, "core", core_count)
    owner = tile_row // per_dev
    slope_index = (
        (owner % core_count) * (pair_count * per_dev)
        + (owner // core_count) * per_dev
        + tile_row % per_dev
    )
    column_part = tile_products(
        tile_values, slope_index, tile_col, count, slope_full, col_tiles, False
    )
    grad_nodes = scatter_sum(column_part, "row", row_count).astype(jnp.bfloat16)
    grad_features = lax.dot_general(
        grad_nodes, weight, (((1,), (1,)), ((), ())), preferred_element_type=jnp.float32
    ).astype(jnp.bfloat16)
    weight_term = lax.dot_general(
        features, grad_nodes, (((0,), (0,)), ((), ())), preferred_element_type=jnp.float32
    )
    everyone = ("row", "colhi", "core")
    devices = row_count * col_count
    weight_piece = scatter_sum(weight_term, everyone, devices)
    grad_weight = gather_rows(weight_piece, everyone, devices)
    return (activated, grad_features, grad_weight)


def solution(mesh):
    rows, cols = mesh.devices.shape
    fine = Mesh(mesh.devices.reshape(rows, cols // 2, 2), ("row", "colhi", "core"))
    col = ("colhi", "core")
    placed = (
        P((*col, "row"), None),
        P(),
        P(("row", *col), None, None),
        P(("row", *col)),
        P(("row", *col)),
        P("row", col),
        P(("row", *col), None),
    )
    return jax.shard_map(
        body,
        mesh=fine,
        in_specs=placed,
        out_specs=(P(("row", *col), None), P((*col, "row"), None), P()),
        check_vma=False,
    )
```

```python
import functools

import jax
import jax.numpy as jnp
from jax import lax
from jax.experimental import pallas as pl
from jax.experimental.pallas import tpu as pltpu
from jax.sharding import Mesh, PartitionSpec as P


GROUP = 32
CHUNK = 256
UNROLL = 4


def silu_slope(values):
    sigma = jax.nn.sigmoid(values)
    return sigma * (1.0 + values * (1.0 - sigma))


def tile_kernel(count_ref, place_ref, fetch_ref, tiles_ref, src_ref, out_ref, acc_ref, *, forward):
    step = pl.program_id(0)
    tile = tiles_ref.shape[1]
    group = tiles_ref.shape[0]
    out_rows = acc_ref.shape[0]

    @pl.when(step == 0)
    def _():
        def zero(k, carry):
            rows = pl.ds(pl.multiple_of(k * CHUNK, CHUNK), CHUNK)
            acc_ref[rows, :] = jnp.zeros((CHUNK, acc_ref.shape[1]), jnp.float32)
            return carry

        lax.fori_loop(0, out_rows // CHUNK, zero, 0)

    base = step * group
    live = jnp.clip(count_ref[0] - base, 0, group)

    def product(slot, j):
        src_rows = pl.ds(pl.multiple_of(fetch_ref[slot] * tile, tile), tile)
        block = tiles_ref[j]
        src = src_ref[src_rows, :]
        if forward:
            return jnp.dot(block, src, preferred_element_type=jnp.float32)
        return lax.dot_general(
            block, src, (((0,), (0,)), ((), ())), preferred_element_type=jnp.float32
        )

    def add(slot, prod):
        dst_rows = pl.ds(pl.multiple_of(place_ref[slot] * tile, tile), tile)
        acc_ref[dst_rows, :] += prod

    def many(k, carry):
        j0 = k * UNROLL
        prods = [product(base + j0 + u, j0 + u) for u in range(UNROLL)]
        for u in range(UNROLL):
            add(base + j0 + u, prods[u])
        return carry

    def one(j, carry):
        add(base + j, product(base + j, j))
        return carry

    full = live // UNROLL
    lax.fori_loop(0, full, many, 0)
    lax.fori_loop(full * UNROLL, live, one, 0)

    @pl.when(step == pl.num_programs(0) - 1)
    def _():
        def emit(k, carry):
            rows = pl.ds(pl.multiple_of(k * CHUNK, CHUNK), CHUNK)
            out_ref[rows, :] = acc_ref[rows, :].astype(out_ref.dtype)
            return carry

        lax.fori_loop(0, out_rows // CHUNK, emit, 0)


def tile_products(tile_values, fetch_index, place_index, count, source, out_tiles, forward):
    slots, tile, _ = tile_values.shape
    hidden = source.shape[-1]
    src_rows = source.shape[0]
    out_rows = out_tiles * tile
    group = GROUP
    steps = slots // group

    def tiles_map(i, count_ref, place_ref, fetch_ref):
        last = jnp.maximum(count_ref[0] - 1, 0) // group
        return (jnp.minimum(i, last), 0, 0)

    grid_spec = pltpu.PrefetchScalarGridSpec(
        num_scalar_prefetch=3,
        grid=(steps,),
        in_specs=[
            pl.BlockSpec((group, tile, tile), tiles_map),
            pl.BlockSpec((src_rows, hidden), lambda i, *_: (0, 0)),
        ],
        out_specs=pl.BlockSpec((out_rows, hidden), lambda i, *_: (0, 0)),
        scratch_shapes=[pltpu.VMEM((out_rows, hidden), jnp.float32)],
    )
    flops = 2 * slots * tile * tile * hidden
    return pl.pallas_call(
        functools.partial(tile_kernel, forward=forward),
        grid_spec=grid_spec,
        out_shape=jax.ShapeDtypeStruct((out_rows, hidden), jnp.bfloat16),
        compiler_params=pltpu.CompilerParams(
            dimension_semantics=("arbitrary",), vmem_limit_bytes=48 * 1024 * 1024
        ),
        cost_estimate=pl.CostEstimate(
            flops=flops,
            bytes_accessed=slots * tile * tile * 2 + src_rows * hidden * 2 + out_rows * hidden * 2,
            transcendentals=0,
        ),
    )(count, place_index, fetch_index, tile_values, source)


def gather_rows(values, axes, parts):
    copies = jnp.broadcast_to(values[None], (parts,) + values.shape)
    return lax.all_to_all(copies, axes, 0, 0, tiled=True).reshape(-1, values.shape[-1])


def scatter_sum(values, axes, parts):
    pieces = lax.all_to_all(values.reshape(parts, -1, values.shape[-1]), axes, 0, 0, tiled=False)
    return pieces.astype(jnp.float32).sum(0)


def body(features, weight, tile_values, tile_row, tile_col, tile_count, cotangent):
    row_count = lax.axis_size("row")
    pair_count = lax.axis_size("colhi")
    core_count = lax.axis_size("core")
    col_count = pair_count * core_count
    node_dev = features.shape[0]
    hidden = features.shape[1]
    tile_size = tile_values.shape[1]
    per_dev = node_dev // tile_size
    row_tiles = node_dev * col_count // tile_size
    col_tiles = node_dev * row_count // tile_size
    count = tile_count.reshape(1)
    projected = jnp.dot(features, weight, preferred_element_type=jnp.float32).astype(jnp.bfloat16)
    panel_rows = gather_rows(projected, "row", row_count)
    forward_part = tile_products(
        tile_values, tile_col, tile_row, count, panel_rows, row_tiles, True
    )
    core = lax.axis_index("core")
    swap = [(0, 1), (1, 0)]
    by_core = forward_part.reshape(pair_count, core_count, node_dev, hidden)
    keep = lax.dynamic_index_in_dim(by_core, core, 1, keepdims=False)
    give = lax.dynamic_index_in_dim(by_core, 1 - core, 1, keepdims=False)
    got = lax.ppermute(give, "core", swap)
    chip_sum = (keep.astype(jnp.float32) + got.astype(jnp.float32)).astype(jnp.bfloat16)
    summed = scatter_sum(chip_sum, "colhi", pair_count)
    activated = jax.nn.silu(summed).astype(jnp.bfloat16)
    slope = (cotangent.astype(jnp.float32) * silu_slope(summed)).astype(jnp.bfloat16)
    slope_pairs = gather_rows(slope, "colhi", pair_count)
    slope_full = jnp.concatenate([slope_pairs, lax.ppermute(slope_pairs, "core", swap)], axis=0)
    owner = tile_row // per_dev
    slope_index = (
        (owner % core_count != core).astype(jnp.int32) * (pair_count * per_dev)
        + (owner // core_count) * per_dev
        + tile_row % per_dev
    )
    column_part = tile_products(
        tile_values, slope_index, tile_col, count, slope_full, col_tiles, False
    )
    grad_nodes = scatter_sum(column_part, "row", row_count).astype(jnp.bfloat16)
    grad_features = lax.dot_general(
        grad_nodes, weight, (((1,), (1,)), ((), ())), preferred_element_type=jnp.float32
    ).astype(jnp.bfloat16)
    weight_term = lax.dot_general(
        features, grad_nodes, (((0,), (0,)), ((), ())), preferred_element_type=jnp.float32
    )
    everyone = ("row", "colhi", "core")
    devices = row_count * col_count
    weight_piece = scatter_sum(weight_term, everyone, devices)
    grad_weight = gather_rows(weight_piece, everyone, devices)
    return (activated, grad_features, grad_weight)


def solution(mesh):
    rows, cols = mesh.devices.shape
    fine = Mesh(mesh.devices.reshape(rows, cols // 2, 2), ("row", "colhi", "core"))
    col = ("colhi", "core")
    placed = (
        P((*col, "row"), None),
        P(),
        P(("row", *col), None, None),
        P(("row", *col)),
        P(("row", *col)),
        P("row", col),
        P(("row", *col), None),
    )
    return jax.shard_map(
        body,
        mesh=fine,
        in_specs=placed,
        out_specs=(P(("row", *col), None), P((*col, "row"), None), P()),
        check_vma=False,
    )
```

```python
import functools

import jax
import jax.numpy as jnp
from jax import lax
from jax.experimental import pallas as pl
from jax.experimental.pallas import tpu as pltpu
from jax.sharding import Mesh, PartitionSpec as P


GROUP = 64
CHUNK = 256
UNROLL = (32, 8, 1)


def silu_slope(values):
    sigma = jax.nn.sigmoid(values)
    return sigma * (1.0 + values * (1.0 - sigma))


def tile_kernel(count_ref, place_ref, fetch_ref, tiles_ref, src_ref, out_ref, acc_ref, *, forward):
    step = pl.program_id(0)
    tile = tiles_ref.shape[1]
    group = tiles_ref.shape[0]
    out_rows = acc_ref.shape[0]

    @pl.when(step == 0)
    def _():
        def zero(k, carry):
            rows = pl.ds(pl.multiple_of(k * CHUNK, CHUNK), CHUNK)
            acc_ref[rows, :] = jnp.zeros((CHUNK, acc_ref.shape[1]), jnp.float32)
            return carry

        lax.fori_loop(0, out_rows // CHUNK, zero, 0)

    base = step * group
    live = jnp.clip(count_ref[0] - base, 0, group)

    def product(slot, j):
        src_rows = pl.ds(pl.multiple_of(fetch_ref[slot] * tile, tile), tile)
        block = tiles_ref[j]
        src = src_ref[src_rows, :]
        if forward:
            return jnp.dot(block, src, preferred_element_type=jnp.float32)
        return lax.dot_general(
            block, src, (((0,), (0,)), ((), ())), preferred_element_type=jnp.float32
        )

    def add(slot, prod):
        dst_rows = pl.ds(pl.multiple_of(place_ref[slot] * tile, tile), tile)
        acc_ref[dst_rows, :] += prod

    def run(start, stop, width):
        def chunk(k, carry):
            j0 = start + k * width
            prods = [product(base + j0 + u, j0 + u) for u in range(width)]
            for u in range(width):
                add(base + j0 + u, prods[u])
            return carry

        chunks = (stop - start) // width
        lax.fori_loop(0, chunks, chunk, 0)
        return start + chunks * width

    done = 0
    for width in UNROLL:
        done = run(done, live, width)

    @pl.when(step == pl.num_programs(0) - 1)
    def _():
        def emit(k, carry):
            rows = pl.ds(pl.multiple_of(k * CHUNK, CHUNK), CHUNK)
            out_ref[rows, :] = acc_ref[rows, :].astype(out_ref.dtype)
            return carry

        lax.fori_loop(0, out_rows // CHUNK, emit, 0)


def tile_products(tile_values, fetch_index, place_index, count, source, out_tiles, forward):
    slots, tile, _ = tile_values.shape
    hidden = source.shape[-1]
    src_rows = source.shape[0]
    out_rows = out_tiles * tile
    group = GROUP
    steps = slots // group

    def tiles_map(i, count_ref, place_ref, fetch_ref):
        last = jnp.maximum(count_ref[0] - 1, 0) // group
        return (jnp.minimum(i, last), 0, 0)

    grid_spec = pltpu.PrefetchScalarGridSpec(
        num_scalar_prefetch=3,
        grid=(steps,),
        in_specs=[
            pl.BlockSpec((group, tile, tile), tiles_map),
            pl.BlockSpec((src_rows, hidden), lambda i, *_: (0, 0)),
        ],
        out_specs=pl.BlockSpec((out_rows, hidden), lambda i, *_: (0, 0)),
        scratch_shapes=[pltpu.VMEM((out_rows, hidden), jnp.float32)],
    )
    flops = 2 * slots * tile * tile * hidden
    return pl.pallas_call(
        functools.partial(tile_kernel, forward=forward),
        grid_spec=grid_spec,
        out_shape=jax.ShapeDtypeStruct((out_rows, hidden), jnp.bfloat16),
        compiler_params=pltpu.CompilerParams(
            dimension_semantics=("arbitrary",), vmem_limit_bytes=48 * 1024 * 1024
        ),
        cost_estimate=pl.CostEstimate(
            flops=flops,
            bytes_accessed=slots * tile * tile * 2 + src_rows * hidden * 2 + out_rows * hidden * 2,
            transcendentals=0,
        ),
    )(count, place_index, fetch_index, tile_values, source)


def gather_rows(values, axes, parts):
    copies = jnp.broadcast_to(values[None], (parts,) + values.shape)
    return lax.all_to_all(copies, axes, 0, 0, tiled=True).reshape(-1, values.shape[-1])


def scatter_sum(values, axes, parts):
    pieces = lax.all_to_all(values.reshape(parts, -1, values.shape[-1]), axes, 0, 0, tiled=False)
    return pieces.astype(jnp.float32).sum(0)


def body(features, weight, tile_values, tile_row, tile_col, tile_count, cotangent):
    row_count = lax.axis_size("row")
    pair_count = lax.axis_size("colhi")
    core_count = lax.axis_size("core")
    col_count = pair_count * core_count
    node_dev = features.shape[0]
    hidden = features.shape[1]
    tile_size = tile_values.shape[1]
    per_dev = node_dev // tile_size
    row_tiles = node_dev * col_count // tile_size
    col_tiles = node_dev * row_count // tile_size
    count = tile_count.reshape(1)
    projected = jnp.dot(features, weight, preferred_element_type=jnp.float32).astype(jnp.bfloat16)
    panel_rows = gather_rows(projected, "row", row_count)
    forward_part = tile_products(
        tile_values, tile_col, tile_row, count, panel_rows, row_tiles, True
    )
    core = lax.axis_index("core")
    swap = [(0, 1), (1, 0)]
    by_core = forward_part.reshape(pair_count, core_count, node_dev, hidden)
    keep = lax.dynamic_index_in_dim(by_core, core, 1, keepdims=False)
    give = lax.dynamic_index_in_dim(by_core, 1 - core, 1, keepdims=False)
    got = lax.ppermute(give, "core", swap)
    chip_sum = (keep.astype(jnp.float32) + got.astype(jnp.float32)).astype(jnp.bfloat16)
    summed = scatter_sum(chip_sum, "colhi", pair_count)
    activated = jax.nn.silu(summed).astype(jnp.bfloat16)
    slope = (cotangent.astype(jnp.float32) * silu_slope(summed)).astype(jnp.bfloat16)
    slope_pairs = gather_rows(slope, "colhi", pair_count)
    slope_full = jnp.concatenate([slope_pairs, lax.ppermute(slope_pairs, "core", swap)], axis=0)
    owner = tile_row // per_dev
    slope_index = (
        (owner % core_count != core).astype(jnp.int32) * (pair_count * per_dev)
        + (owner // core_count) * per_dev
        + tile_row % per_dev
    )
    column_part = tile_products(
        tile_values, slope_index, tile_col, count, slope_full, col_tiles, False
    )
    grad_nodes = scatter_sum(column_part, "row", row_count).astype(jnp.bfloat16)
    grad_features = lax.dot_general(
        grad_nodes, weight, (((1,), (1,)), ((), ())), preferred_element_type=jnp.float32
    ).astype(jnp.bfloat16)
    weight_term = lax.dot_general(
        features, grad_nodes, (((0,), (0,)), ((), ())), preferred_element_type=jnp.float32
    )
    everyone = ("row", "colhi", "core")
    devices = row_count * col_count
    weight_piece = scatter_sum(weight_term, everyone, devices)
    grad_weight = gather_rows(weight_piece, everyone, devices)
    return (activated, grad_features, grad_weight)


def solution(mesh):
    rows, cols = mesh.devices.shape
    fine = Mesh(mesh.devices.reshape(rows, cols // 2, 2), ("row", "colhi", "core"))
    col = ("colhi", "core")
    placed = (
        P((*col, "row"), None),
        P(),
        P(("row", *col), None, None),
        P(("row", *col)),
        P(("row", *col)),
        P("row", col),
        P(("row", *col), None),
    )
    return jax.shard_map(
        body,
        mesh=fine,
        in_specs=placed,
        out_specs=(P(("row", *col), None), P((*col, "row"), None), P()),
        check_vma=False,
    )
```

```python
import functools

import jax
import jax.numpy as jnp
from jax import lax
from jax.experimental import pallas as pl
from jax.experimental.pallas import tpu as pltpu
from jax.sharding import Mesh, PartitionSpec as P


GROUP = 64
CHUNK = 256
UNROLL = (32, 8, 1)


def silu_slope(values):
    sigma = jax.nn.sigmoid(values)
    return sigma * (1.0 + values * (1.0 - sigma))


def tile_kernel(count_ref, place_ref, fetch_ref, tiles_ref, src_ref, out_ref, acc_ref, *, forward):
    step = pl.program_id(0)
    tile = tiles_ref.shape[1]
    group = tiles_ref.shape[0]
    out_rows = acc_ref.shape[0]

    @pl.when(step == 0)
    def _():
        def zero(k, carry):
            rows = pl.ds(pl.multiple_of(k * CHUNK, CHUNK), CHUNK)
            acc_ref[rows, :] = jnp.zeros((CHUNK, acc_ref.shape[1]), jnp.float32)
            return carry

        lax.fori_loop(0, out_rows // CHUNK, zero, 0)

    base = step * group
    live = jnp.clip(count_ref[0] - base, 0, group)

    def product(slot, j):
        src_rows = pl.ds(pl.multiple_of(fetch_ref[slot] * tile, tile), tile)
        block = tiles_ref[j]
        src = src_ref[src_rows, :]
        if forward:
            return jnp.dot(block, src, preferred_element_type=jnp.float32)
        return lax.dot_general(
            block, src, (((0,), (0,)), ((), ())), preferred_element_type=jnp.float32
        )

    def add(slot, prod):
        dst_rows = pl.ds(pl.multiple_of(place_ref[slot] * tile, tile), tile)
        acc_ref[dst_rows, :] += prod

    def run(start, stop, width):
        def chunk(k, carry):
            j0 = start + k * width
            prods = [product(base + j0 + u, j0 + u) for u in range(width)]
            for u in range(width):
                add(base + j0 + u, prods[u])
            return carry

        chunks = (stop - start) // width
        lax.fori_loop(0, chunks, chunk, 0)
        return start + chunks * width

    done = 0
    for width in UNROLL:
        done = run(done, live, width)

    @pl.when(step == pl.num_programs(0) - 1)
    def _():
        def emit(k, carry):
            rows = pl.ds(pl.multiple_of(k * CHUNK, CHUNK), CHUNK)
            out_ref[rows, :] = acc_ref[rows, :].astype(out_ref.dtype)
            return carry

        lax.fori_loop(0, out_rows // CHUNK, emit, 0)


def tile_products(tile_values, fetch_index, place_index, count, source, out_tiles, forward):
    slots, tile, _ = tile_values.shape
    hidden = source.shape[-1]
    src_rows = source.shape[0]
    out_rows = out_tiles * tile
    group = GROUP
    steps = slots // group

    def tiles_map(i, count_ref, place_ref, fetch_ref):
        last = jnp.maximum(count_ref[0] - 1, 0) // group
        return (jnp.minimum(i, last), 0, 0)

    grid_spec = pltpu.PrefetchScalarGridSpec(
        num_scalar_prefetch=3,
        grid=(steps,),
        in_specs=[
            pl.BlockSpec((group, tile, tile), tiles_map),
            pl.BlockSpec((src_rows, hidden), lambda i, *_: (0, 0)),
        ],
        out_specs=pl.BlockSpec((out_rows, hidden), lambda i, *_: (0, 0)),
        scratch_shapes=[pltpu.VMEM((out_rows, hidden), jnp.float32)],
    )
    flops = 2 * slots * tile * tile * hidden
    return pl.pallas_call(
        functools.partial(tile_kernel, forward=forward),
        grid_spec=grid_spec,
        out_shape=jax.ShapeDtypeStruct((out_rows, hidden), jnp.bfloat16),
        compiler_params=pltpu.CompilerParams(
            dimension_semantics=("arbitrary",), vmem_limit_bytes=48 * 1024 * 1024
        ),
        cost_estimate=pl.CostEstimate(
            flops=flops,
            bytes_accessed=slots * tile * tile * 2 + src_rows * hidden * 2 + out_rows * hidden * 2,
            transcendentals=0,
        ),
    )(count, place_index, fetch_index, tile_values, source)


MESH = pl.DeviceIdType.MESH
AXES = ("row", "colhi", "core")


def exchange_kernel(src_ref, dst_ref, send_sem, recv_sem, local_sem, *, axis, parts, gather):
    me = lax.axis_index(axis)

    def device(peer):
        return tuple(peer if name == axis else lax.axis_index(name) for name in AXES)

    barrier = pltpu.get_barrier_semaphore()
    for k in range(1, parts):
        peer = lax.rem(me + k, parts)
        pl.semaphore_signal(barrier, inc=1, device_id=device(peer), device_id_type=MESH)
    pl.semaphore_wait(barrier, parts - 1)

    local = pltpu.make_async_copy(src_ref if gather else src_ref.at[me], dst_ref.at[me], local_sem)
    local.start()
    sends = []
    for k in range(1, parts):
        peer = lax.rem(me + k, parts)
        copy = pltpu.make_async_remote_copy(
            src_ref=src_ref if gather else src_ref.at[peer],
            dst_ref=dst_ref.at[me],
            send_sem=send_sem.at[k],
            recv_sem=recv_sem.at[k],
            device_id=device(peer),
            device_id_type=MESH,
        )
        copy.start()
        sends.append(copy)
    for k in range(1, parts):
        source = lax.rem(me + parts - k, parts)
        incoming = pltpu.make_async_remote_copy(
            src_ref=src_ref if gather else src_ref.at[source],
            dst_ref=dst_ref.at[source],
            send_sem=send_sem.at[k],
            recv_sem=recv_sem.at[k],
            device_id=device(source),
            device_id_type=MESH,
        )
        incoming.wait_recv()
    for copy in sends:
        copy.wait_send()
    local.wait()


def exchange(values, axis, parts, gather, tag):
    block = values.shape if gather else values.shape[1:]
    return pl.pallas_call(
        functools.partial(exchange_kernel, axis=axis, parts=parts, gather=gather),
        out_shape=jax.ShapeDtypeStruct((parts,) + block, values.dtype),
        in_specs=[pl.BlockSpec(memory_space=pl.ANY)],
        out_specs=pl.BlockSpec(memory_space=pl.ANY),
        scratch_shapes=[
            pltpu.SemaphoreType.DMA((parts,)),
            pltpu.SemaphoreType.DMA((parts,)),
            pltpu.SemaphoreType.DMA,
        ],
        compiler_params=pltpu.CompilerParams(collective_id=tag, has_side_effects=True),
    )(values)


def gather_rows(values, axes, parts):
    copies = jnp.broadcast_to(values[None], (parts,) + values.shape)
    return lax.all_to_all(copies, axes, 0, 0, tiled=True).reshape(-1, values.shape[-1])


def scatter_sum(values, axes, parts):
    pieces = lax.all_to_all(values.reshape(parts, -1, values.shape[-1]), axes, 0, 0, tiled=False)
    return pieces.astype(jnp.float32).sum(0)


def body(features, weight, tile_values, tile_row, tile_col, tile_count, cotangent):
    row_count = lax.axis_size("row")
    pair_count = lax.axis_size("colhi")
    core_count = lax.axis_size("core")
    col_count = pair_count * core_count
    node_dev = features.shape[0]
    hidden = features.shape[1]
    tile_size = tile_values.shape[1]
    per_dev = node_dev // tile_size
    row_tiles = node_dev * col_count // tile_size
    col_tiles = node_dev * row_count // tile_size
    count = tile_count.reshape(1)
    projected = jnp.dot(features, weight, preferred_element_type=jnp.float32).astype(jnp.bfloat16)
    panel_rows = gather_rows(projected, "row", row_count)
    forward_part = tile_products(
        tile_values, tile_col, tile_row, count, panel_rows, row_tiles, True
    )
    core = lax.axis_index("core")
    swap = [(0, 1), (1, 0)]
    by_core = forward_part.reshape(pair_count, core_count, node_dev, hidden)
    keep = lax.dynamic_index_in_dim(by_core, core, 1, keepdims=False)
    give = lax.dynamic_index_in_dim(by_core, 1 - core, 1, keepdims=False)
    got = lax.ppermute(give, "core", swap)
    chip_sum = (keep.astype(jnp.float32) + got.astype(jnp.float32)).astype(jnp.bfloat16)
    summed = exchange(
        chip_sum.reshape(pair_count, node_dev, hidden), "colhi", pair_count, False, 0
    ).astype(jnp.float32).sum(0)
    activated = jax.nn.silu(summed).astype(jnp.bfloat16)
    slope = (cotangent.astype(jnp.float32) * silu_slope(summed)).astype(jnp.bfloat16)
    slope_pairs = exchange(slope, "colhi", pair_count, True, 1).reshape(-1, hidden)
    slope_full = jnp.concatenate([slope_pairs, lax.ppermute(slope_pairs, "core", swap)], axis=0)
    owner = tile_row // per_dev
    slope_index = (
        (owner % core_count != core).astype(jnp.int32) * (pair_count * per_dev)
        + (owner // core_count) * per_dev
        + tile_row % per_dev
    )
    column_part = tile_products(
        tile_values, slope_index, tile_col, count, slope_full, col_tiles, False
    )
    grad_nodes = scatter_sum(column_part, "row", row_count).astype(jnp.bfloat16)
    grad_features = lax.dot_general(
        grad_nodes, weight, (((1,), (1,)), ((), ())), preferred_element_type=jnp.float32
    ).astype(jnp.bfloat16)
    weight_term = lax.dot_general(
        features, grad_nodes, (((0,), (0,)), ((), ())), preferred_element_type=jnp.float32
    )
    everyone = ("row", "colhi", "core")
    devices = row_count * col_count
    weight_piece = scatter_sum(weight_term, everyone, devices)
    grad_weight = gather_rows(weight_piece, everyone, devices)
    return (activated, grad_features, grad_weight)


def solution(mesh):
    rows, cols = mesh.devices.shape
    fine = Mesh(mesh.devices.reshape(rows, cols // 2, 2), ("row", "colhi", "core"))
    col = ("colhi", "core")
    placed = (
        P((*col, "row"), None),
        P(),
        P(("row", *col), None, None),
        P(("row", *col)),
        P(("row", *col)),
        P("row", col),
        P(("row", *col), None),
    )
    return jax.shard_map(
        body,
        mesh=fine,
        in_specs=placed,
        out_specs=(P(("row", *col), None), P((*col, "row"), None), P()),
        check_vma=False,
    )
```

```python
import functools

import jax
import jax.numpy as jnp
from jax import lax
from jax.experimental import pallas as pl
from jax.experimental.pallas import tpu as pltpu
from jax.sharding import Mesh, PartitionSpec as P


GROUP = 64
CHUNK = 256
UNROLL = (64, 8, 1)


def silu_slope(values):
    sigma = jax.nn.sigmoid(values)
    return sigma * (1.0 + values * (1.0 - sigma))


def tile_kernel(count_ref, place_ref, fetch_ref, tiles_ref, src_ref, *refs, forward, block_rows):
    if block_rows:
        keep_ref, give_ref, acc_ref = refs
    else:
        out_ref, acc_ref = refs
    step = pl.program_id(0)
    tile = tiles_ref.shape[1]
    group = tiles_ref.shape[0]
    out_rows = acc_ref.shape[0]

    @pl.when(step == 0)
    def _():
        def zero(k, carry):
            rows = pl.ds(pl.multiple_of(k * CHUNK, CHUNK), CHUNK)
            acc_ref[rows, :] = jnp.zeros((CHUNK, acc_ref.shape[1]), jnp.float32)
            return carry

        lax.fori_loop(0, out_rows // CHUNK, zero, 0)

    base = step * group
    live = jnp.clip(count_ref[0] - base, 0, group)

    def product(slot, j):
        src_rows = pl.ds(pl.multiple_of(fetch_ref[slot] * tile, tile), tile)
        block = tiles_ref[j]
        src = src_ref[src_rows, :]
        if forward:
            return jnp.dot(block, src, preferred_element_type=jnp.float32)
        return lax.dot_general(
            block, src, (((0,), (0,)), ((), ())), preferred_element_type=jnp.float32
        )

    def add(slot, prod):
        dst_rows = pl.ds(pl.multiple_of(place_ref[slot] * tile, tile), tile)
        acc_ref[dst_rows, :] += prod

    def run(start, stop, width):
        def chunk(k, carry):
            j0 = start + k * width
            prods = [product(base + j0 + u, j0 + u) for u in range(width)]
            for u in range(width):
                add(base + j0 + u, prods[u])
            return carry

        chunks = (stop - start) // width
        lax.fori_loop(0, chunks, chunk, 0)
        return start + chunks * width

    done = 0
    for width in UNROLL:
        done = run(done, live, width)

    @pl.when(step == pl.num_programs(0) - 1)
    def _():
        def emit(k, carry):
            rows = pl.ds(pl.multiple_of(k * CHUNK, CHUNK), CHUNK)
            if not block_rows:
                out_ref[rows, :] = acc_ref[rows, :].astype(out_ref.dtype)
                return carry
            values = acc_ref[rows, :].astype(keep_ref.dtype)
            block = k * CHUNK // block_rows
            dst = pl.ds(
                pl.multiple_of((block // 2) * block_rows + k * CHUNK % block_rows, CHUNK), CHUNK
            )

            @pl.when(block % 2 == count_ref[1])
            def _():
                keep_ref[dst, :] = values

            @pl.when(block % 2 != count_ref[1])
            def _():
                give_ref[dst, :] = values

            return carry

        lax.fori_loop(0, out_rows // CHUNK, emit, 0)


def tile_products(tile_values, fetch_index, place_index, count, source, out_tiles, forward, block_rows=0):
    slots, tile, _ = tile_values.shape
    hidden = source.shape[-1]
    src_rows = source.shape[0]
    out_rows = out_tiles * tile
    group = GROUP
    steps = slots // group

    def tiles_map(i, count_ref, place_ref, fetch_ref):
        last = jnp.maximum(count_ref[0] - 1, 0) // group
        return (jnp.minimum(i, last), 0, 0)

    grid_spec = pltpu.PrefetchScalarGridSpec(
        num_scalar_prefetch=3,
        grid=(steps,),
        in_specs=[
            pl.BlockSpec((group, tile, tile), tiles_map),
            pl.BlockSpec((src_rows, hidden), lambda i, *_: (0, 0)),
        ],
        out_specs=[pl.BlockSpec((out_rows // 2, hidden), lambda i, *_: (0, 0))] * 2
        if block_rows
        else pl.BlockSpec((out_rows, hidden), lambda i, *_: (0, 0)),
        scratch_shapes=[pltpu.VMEM((out_rows, hidden), jnp.float32)],
    )
    flops = 2 * slots * tile * tile * hidden
    return pl.pallas_call(
        functools.partial(tile_kernel, forward=forward, block_rows=block_rows),
        grid_spec=grid_spec,
        out_shape=[jax.ShapeDtypeStruct((out_rows // 2, hidden), jnp.bfloat16)] * 2
        if block_rows
        else jax.ShapeDtypeStruct((out_rows, hidden), jnp.bfloat16),
        compiler_params=pltpu.CompilerParams(
            dimension_semantics=("arbitrary",), vmem_limit_bytes=48 * 1024 * 1024
        ),
        cost_estimate=pl.CostEstimate(
            flops=flops,
            bytes_accessed=slots * tile * tile * 2 + src_rows * hidden * 2 + out_rows * hidden * 2,
            transcendentals=0,
        ),
    )(count, place_index, fetch_index, tile_values, source)


def gather_rows(values, axes, parts):
    copies = jnp.broadcast_to(values[None], (parts,) + values.shape)
    return lax.all_to_all(copies, axes, 0, 0, tiled=True).reshape(-1, values.shape[-1])


def scatter_sum(values, axes, parts):
    pieces = lax.all_to_all(values.reshape(parts, -1, values.shape[-1]), axes, 0, 0, tiled=False)
    return pieces.astype(jnp.float32).sum(0)


def body(features, weight, tile_values, tile_row, tile_col, tile_count, cotangent):
    row_count = lax.axis_size("row")
    pair_count = lax.axis_size("colhi")
    core_count = lax.axis_size("core")
    col_count = pair_count * core_count
    node_dev = features.shape[0]
    hidden = features.shape[1]
    tile_size = tile_values.shape[1]
    per_dev = node_dev // tile_size
    row_tiles = node_dev * col_count // tile_size
    col_tiles = node_dev * row_count // tile_size
    core = lax.axis_index("core")
    count = jnp.stack([tile_count.reshape(()), core.astype(jnp.int32)])
    projected = jnp.dot(features, weight, preferred_element_type=jnp.float32).astype(jnp.bfloat16)
    panel_rows = gather_rows(projected, "row", row_count)
    swap = [(0, 1), (1, 0)]
    keep, give = tile_products(
        tile_values, tile_col, tile_row, count, panel_rows, row_tiles, True, node_dev
    )
    got = lax.ppermute(give, "core", swap)
    chip_sum = (keep.astype(jnp.float32) + got.astype(jnp.float32)).astype(jnp.bfloat16)
    chip_sum = chip_sum.reshape(pair_count, node_dev, hidden)
    summed = scatter_sum(chip_sum, "colhi", pair_count)
    activated = jax.nn.silu(summed).astype(jnp.bfloat16)
    slope = (cotangent.astype(jnp.float32) * silu_slope(summed)).astype(jnp.bfloat16)
    slope_pairs = gather_rows(slope, "colhi", pair_count)
    slope_full = jnp.concatenate([slope_pairs, lax.ppermute(slope_pairs, "core", swap)], axis=0)
    owner = tile_row // per_dev
    slope_index = (
        (owner % core_count != core).astype(jnp.int32) * (pair_count * per_dev)
        + (owner // core_count) * per_dev
        + tile_row % per_dev
    )
    column_part = tile_products(
        tile_values, slope_index, tile_col, count, slope_full, col_tiles, False
    )
    grad_nodes = scatter_sum(column_part, "row", row_count).astype(jnp.bfloat16)
    grad_features = lax.dot_general(
        grad_nodes, weight, (((1,), (1,)), ((), ())), preferred_element_type=jnp.float32
    ).astype(jnp.bfloat16)
    weight_term = lax.dot_general(
        features, grad_nodes, (((0,), (0,)), ((), ())), preferred_element_type=jnp.float32
    )
    everyone = ("row", "colhi", "core")
    devices = row_count * col_count
    weight_piece = scatter_sum(weight_term, everyone, devices)
    grad_weight = gather_rows(weight_piece, everyone, devices)
    return (activated, grad_features, grad_weight)


def solution(mesh):
    rows, cols = mesh.devices.shape
    fine = Mesh(mesh.devices.reshape(rows, cols // 2, 2), ("row", "colhi", "core"))
    col = ("colhi", "core")
    placed = (
        P((*col, "row"), None),
        P(),
        P(("row", *col), None, None),
        P(("row", *col)),
        P(("row", *col)),
        P("row", col),
        P(("row", *col), None),
    )
    return jax.shard_map(
        body,
        mesh=fine,
        in_specs=placed,
        out_specs=(P(("row", *col), None), P((*col, "row"), None), P()),
        check_vma=False,
    )
```

```python
import functools

import jax
import jax.numpy as jnp
from jax import lax
from jax.experimental import pallas as pl
from jax.experimental.pallas import tpu as pltpu
from jax.sharding import Mesh, PartitionSpec as P


GROUP = 64
CHUNK = 256
UNROLL = (64, 8, 1)


def silu_slope(values):
    sigma = jax.nn.sigmoid(values)
    return sigma * (1.0 + values * (1.0 - sigma))


def tile_kernel(count_ref, place_ref, fetch_ref, tiles_ref, src_ref, *refs, forward, block_rows):
    if block_rows:
        keep_ref, give_ref, acc_ref = refs
    else:
        out_ref, acc_ref = refs
    step = pl.program_id(0)
    tile = tiles_ref.shape[1]
    group = tiles_ref.shape[0]
    out_rows = acc_ref.shape[0]

    @pl.when(step == 0)
    def _():
        def zero(k, carry):
            rows = pl.ds(pl.multiple_of(k * CHUNK, CHUNK), CHUNK)
            acc_ref[rows, :] = jnp.zeros((CHUNK, acc_ref.shape[1]), jnp.float32)
            return carry

        lax.fori_loop(0, out_rows // CHUNK, zero, 0)

    base = step * group
    live = jnp.clip(count_ref[0] - base, 0, group)

    def product(slot, j):
        src_rows = pl.ds(pl.multiple_of(fetch_ref[slot] * tile, tile), tile)
        block = tiles_ref[j]
        src = src_ref[src_rows, :]
        if forward:
            return jnp.dot(block, src, preferred_element_type=jnp.float32)
        return lax.dot_general(
            block, src, (((0,), (0,)), ((), ())), preferred_element_type=jnp.float32
        )

    def add(slot, prod):
        dst_rows = pl.ds(pl.multiple_of(place_ref[slot] * tile, tile), tile)
        acc_ref[dst_rows, :] += prod

    def run(start, stop, width):
        def chunk(k, carry):
            j0 = start + k * width
            prods = [product(base + j0 + u, j0 + u) for u in range(width)]
            for u in range(width):
                add(base + j0 + u, prods[u])
            return carry

        chunks = (stop - start) // width
        lax.fori_loop(0, chunks, chunk, 0)
        return start + chunks * width

    done = 0
    for width in UNROLL:
        done = run(done, live, width)

    @pl.when(step == pl.num_programs(0) - 1)
    def _():
        def emit(k, carry):
            rows = pl.ds(pl.multiple_of(k * CHUNK, CHUNK), CHUNK)
            if not block_rows:
                out_ref[rows, :] = acc_ref[rows, :].astype(out_ref.dtype)
                return carry
            values = acc_ref[rows, :].astype(keep_ref.dtype)
            block = k * CHUNK // block_rows
            dst = pl.ds(
                pl.multiple_of((block // 2) * block_rows + k * CHUNK % block_rows, CHUNK), CHUNK
            )

            @pl.when(block % 2 == count_ref[1])
            def _():
                keep_ref[dst, :] = values

            @pl.when(block % 2 != count_ref[1])
            def _():
                give_ref[dst, :] = values

            return carry

        lax.fori_loop(0, out_rows // CHUNK, emit, 0)


def tile_products(tile_values, fetch_index, place_index, count, source, out_tiles, forward, block_rows=0):
    slots, tile, _ = tile_values.shape
    hidden = source.shape[-1]
    src_rows = source.shape[0]
    out_rows = out_tiles * tile
    group = GROUP
    steps = slots // group

    def tiles_map(i, count_ref, place_ref, fetch_ref):
        last = jnp.maximum(count_ref[0] - 1, 0) // group
        return (jnp.minimum(i, last), 0, 0)

    grid_spec = pltpu.PrefetchScalarGridSpec(
        num_scalar_prefetch=3,
        grid=(steps,),
        in_specs=[
            pl.BlockSpec((group, tile, tile), tiles_map),
            pl.BlockSpec((src_rows, hidden), lambda i, *_: (0, 0)),
        ],
        out_specs=[pl.BlockSpec((out_rows // 2, hidden), lambda i, *_: (0, 0))] * 2
        if block_rows
        else pl.BlockSpec((out_rows, hidden), lambda i, *_: (0, 0)),
        scratch_shapes=[pltpu.VMEM((out_rows, hidden), jnp.float32)],
    )
    flops = 2 * slots * tile * tile * hidden
    return pl.pallas_call(
        functools.partial(tile_kernel, forward=forward, block_rows=block_rows),
        grid_spec=grid_spec,
        out_shape=[jax.ShapeDtypeStruct((out_rows // 2, hidden), jnp.bfloat16)] * 2
        if block_rows
        else jax.ShapeDtypeStruct((out_rows, hidden), jnp.bfloat16),
        compiler_params=pltpu.CompilerParams(
            dimension_semantics=("arbitrary",), vmem_limit_bytes=48 * 1024 * 1024
        ),
        cost_estimate=pl.CostEstimate(
            flops=flops,
            bytes_accessed=slots * tile * tile * 2 + src_rows * hidden * 2 + out_rows * hidden * 2,
            transcendentals=0,
        ),
    )(count, place_index, fetch_index, tile_values, source)


def gather_rows(values, axes, parts):
    copies = jnp.broadcast_to(values[None], (parts,) + values.shape)
    return lax.all_to_all(copies, axes, 0, 0, tiled=True).reshape(-1, values.shape[-1])


def scatter_sum(values, axes, parts):
    pieces = lax.all_to_all(values.reshape(parts, -1, values.shape[-1]), axes, 0, 0, tiled=False)
    return pieces.astype(jnp.float32).sum(0)


def body(features, weight, tile_values, tile_row, tile_col, tile_count, cotangent):
    row_count = lax.axis_size("row")
    pair_count = lax.axis_size("colhi")
    core_count = lax.axis_size("core")
    col_count = pair_count * core_count
    node_dev = features.shape[0]
    hidden = features.shape[1]
    tile_size = tile_values.shape[1]
    per_dev = node_dev // tile_size
    row_tiles = node_dev * col_count // tile_size
    col_tiles = node_dev * row_count // tile_size
    core = lax.axis_index("core")
    count = jnp.stack([tile_count.reshape(()), core.astype(jnp.int32)])
    features_block = gather_rows(features, "row", row_count)
    panel_rows = jnp.dot(features_block, weight, preferred_element_type=jnp.float32).astype(
        jnp.bfloat16
    )
    swap = [(0, 1), (1, 0)]
    keep, give = tile_products(
        tile_values, tile_col, tile_row, count, panel_rows, row_tiles, True, node_dev
    )
    got = lax.ppermute(give, "core", swap)
    chip_sum = (keep.astype(jnp.float32) + got.astype(jnp.float32)).astype(jnp.bfloat16)
    chip_sum = chip_sum.reshape(pair_count, node_dev, hidden)
    summed = scatter_sum(chip_sum, "colhi", pair_count)
    activated = jax.nn.silu(summed).astype(jnp.bfloat16)
    slope = (cotangent.astype(jnp.float32) * silu_slope(summed)).astype(jnp.bfloat16)
    slope_pairs = gather_rows(slope, "colhi", pair_count)
    slope_full = jnp.concatenate([slope_pairs, lax.ppermute(slope_pairs, "core", swap)], axis=0)
    owner = tile_row // per_dev
    slope_index = (
        (owner % core_count != core).astype(jnp.int32) * (pair_count * per_dev)
        + (owner // core_count) * per_dev
        + tile_row % per_dev
    )
    column_part = tile_products(
        tile_values, slope_index, tile_col, count, slope_full, col_tiles, False
    )
    weight_term = lax.dot_general(
        features_block, column_part, (((0,), (0,)), ((), ())), preferred_element_type=jnp.float32
    )
    term_rows = hidden // row_count
    packed = jnp.concatenate(
        [
            column_part.reshape(row_count, node_dev, hidden),
            weight_term.astype(jnp.bfloat16).reshape(row_count, term_rows, hidden),
        ],
        axis=1,
    )
    reduced = scatter_sum(packed, "row", row_count)
    grad_nodes = reduced[:node_dev].astype(jnp.bfloat16)
    col_terms = gather_rows(reduced[node_dev:], ("colhi", "core"), col_count)
    weight_rows = col_terms.reshape(col_count, term_rows, hidden).sum(0)
    grad_weight = gather_rows(weight_rows, "row", row_count)
    grad_features = lax.dot_general(
        grad_nodes, weight, (((1,), (1,)), ((), ())), preferred_element_type=jnp.float32
    ).astype(jnp.bfloat16)
    return (activated, grad_features, grad_weight)


def solution(mesh):
    rows, cols = mesh.devices.shape
    fine = Mesh(mesh.devices.reshape(rows, cols // 2, 2), ("row", "colhi", "core"))
    col = ("colhi", "core")
    placed = (
        P((*col, "row"), None),
        P(),
        P(("row", *col), None, None),
        P(("row", *col)),
        P(("row", *col)),
        P("row", col),
        P(("row", *col), None),
    )
    return jax.shard_map(
        body,
        mesh=fine,
        in_specs=placed,
        out_specs=(P(("row", *col), None), P((*col, "row"), None), P()),
        check_vma=False,
    )
```

```python
import functools

import jax
import jax.numpy as jnp
from jax import lax
from jax.experimental import pallas as pl
from jax.experimental.pallas import tpu as pltpu
from jax.sharding import Mesh, PartitionSpec as P


GROUP = 64
CHUNK = 256
UNROLL = (64, 8, 1)


def silu_slope(values):
    sigma = jax.nn.sigmoid(values)
    return sigma * (1.0 + values * (1.0 - sigma))


def tile_kernel(count_ref, place_ref, fetch_ref, tiles_ref, src_ref, *refs, forward, block_rows):
    if block_rows:
        keep_ref, give_ref, acc_ref = refs
    else:
        out_ref, acc_ref = refs
    step = pl.program_id(0)
    tile = tiles_ref.shape[1]
    group = tiles_ref.shape[0]
    out_rows = acc_ref.shape[0]

    @pl.when(step == 0)
    def _():
        def zero(k, carry):
            rows = pl.ds(pl.multiple_of(k * CHUNK, CHUNK), CHUNK)
            acc_ref[rows, :] = jnp.zeros((CHUNK, acc_ref.shape[1]), jnp.float32)
            return carry

        lax.fori_loop(0, out_rows // CHUNK, zero, 0)

    base = step * group
    live = jnp.clip(count_ref[0] - base, 0, group)

    def product(slot, j):
        src_rows = pl.ds(pl.multiple_of(fetch_ref[slot] * tile, tile), tile)
        block = tiles_ref[j]
        src = src_ref[src_rows, :]
        if forward:
            return jnp.dot(block, src, preferred_element_type=jnp.float32)
        return lax.dot_general(
            block, src, (((0,), (0,)), ((), ())), preferred_element_type=jnp.float32
        )

    def add(slot, prod):
        dst_rows = pl.ds(pl.multiple_of(place_ref[slot] * tile, tile), tile)
        acc_ref[dst_rows, :] += prod

    def run(start, stop, width):
        def chunk(k, carry):
            j0 = start + k * width
            prods = [product(base + j0 + u, j0 + u) for u in range(width)]
            for u in range(width):
                add(base + j0 + u, prods[u])
            return carry

        chunks = (stop - start) // width
        lax.fori_loop(0, chunks, chunk, 0)
        return start + chunks * width

    done = 0
    for width in UNROLL:
        done = run(done, live, width)

    @pl.when(step == pl.num_programs(0) - 1)
    def _():
        def emit(k, carry):
            rows = pl.ds(pl.multiple_of(k * CHUNK, CHUNK), CHUNK)
            if not block_rows:
                out_ref[rows, :] = acc_ref[rows, :].astype(out_ref.dtype)
                return carry
            values = acc_ref[rows, :].astype(keep_ref.dtype)
            block = k * CHUNK // block_rows
            dst = pl.ds(
                pl.multiple_of((block // 2) * block_rows + k * CHUNK % block_rows, CHUNK), CHUNK
            )

            @pl.when(block % 2 == count_ref[1])
            def _():
                keep_ref[dst, :] = values

            @pl.when(block % 2 != count_ref[1])
            def _():
                give_ref[dst, :] = values

            return carry

        lax.fori_loop(0, out_rows // CHUNK, emit, 0)


def tile_products(tile_values, fetch_index, place_index, count, source, out_tiles, forward, block_rows=0):
    slots, tile, _ = tile_values.shape
    hidden = source.shape[-1]
    src_rows = source.shape[0]
    out_rows = out_tiles * tile
    group = GROUP
    steps = slots // group

    def tiles_map(i, count_ref, place_ref, fetch_ref):
        last = jnp.maximum(count_ref[0] - 1, 0) // group
        return (jnp.minimum(i, last), 0, 0)

    grid_spec = pltpu.PrefetchScalarGridSpec(
        num_scalar_prefetch=3,
        grid=(steps,),
        in_specs=[
            pl.BlockSpec((group, tile, tile), tiles_map),
            pl.BlockSpec((src_rows, hidden), lambda i, *_: (0, 0)),
        ],
        out_specs=[pl.BlockSpec((out_rows // 2, hidden), lambda i, *_: (0, 0))] * 2
        if block_rows
        else pl.BlockSpec((out_rows, hidden), lambda i, *_: (0, 0)),
        scratch_shapes=[pltpu.VMEM((out_rows, hidden), jnp.float32)],
    )
    flops = 2 * slots * tile * tile * hidden
    return pl.pallas_call(
        functools.partial(tile_kernel, forward=forward, block_rows=block_rows),
        grid_spec=grid_spec,
        out_shape=[jax.ShapeDtypeStruct((out_rows // 2, hidden), jnp.bfloat16)] * 2
        if block_rows
        else jax.ShapeDtypeStruct((out_rows, hidden), jnp.bfloat16),
        compiler_params=pltpu.CompilerParams(
            dimension_semantics=("arbitrary",), vmem_limit_bytes=48 * 1024 * 1024
        ),
        cost_estimate=pl.CostEstimate(
            flops=flops,
            bytes_accessed=slots * tile * tile * 2 + src_rows * hidden * 2 + out_rows * hidden * 2,
            transcendentals=0,
        ),
    )(count, place_index, fetch_index, tile_values, source)


MESH = pl.DeviceIdType.MESH
AXES = ("row", "colhi", "core")


def exchange_kernel(src_ref, dst_ref, send_sem, recv_sem, local_sem, *, axis, parts, gather):
    me = lax.axis_index(axis)

    def device(peer):
        return tuple(peer if name == axis else lax.axis_index(name) for name in AXES)

    barrier = pltpu.get_barrier_semaphore()
    for k in range(1, parts):
        peer = lax.rem(me + k, parts)
        pl.semaphore_signal(barrier, inc=1, device_id=device(peer), device_id_type=MESH)
    pl.semaphore_wait(barrier, parts - 1)

    local = pltpu.make_async_copy(src_ref if gather else src_ref.at[me], dst_ref.at[me], local_sem)
    local.start()
    sends = []
    for k in range(1, parts):
        peer = lax.rem(me + k, parts)
        copy = pltpu.make_async_remote_copy(
            src_ref=src_ref if gather else src_ref.at[peer],
            dst_ref=dst_ref.at[me],
            send_sem=send_sem.at[k],
            recv_sem=recv_sem.at[k],
            device_id=device(peer),
            device_id_type=MESH,
        )
        copy.start()
        sends.append(copy)
    for k in range(1, parts):
        source = lax.rem(me + parts - k, parts)
        incoming = pltpu.make_async_remote_copy(
            src_ref=src_ref if gather else src_ref.at[source],
            dst_ref=dst_ref.at[source],
            send_sem=send_sem.at[k],
            recv_sem=recv_sem.at[k],
            device_id=device(source),
            device_id_type=MESH,
        )
        incoming.wait_recv()
    for copy in sends:
        copy.wait_send()
    local.wait()


def exchange(values, axis, parts, gather, tag):
    block = values.shape if gather else values.shape[1:]
    return pl.pallas_call(
        functools.partial(exchange_kernel, axis=axis, parts=parts, gather=gather),
        out_shape=jax.ShapeDtypeStruct((parts,) + block, values.dtype),
        in_specs=[pl.BlockSpec(memory_space=pl.ANY)],
        out_specs=pl.BlockSpec(memory_space=pl.ANY),
        scratch_shapes=[
            pltpu.SemaphoreType.DMA((parts,)),
            pltpu.SemaphoreType.DMA((parts,)),
            pltpu.SemaphoreType.DMA,
        ],
        compiler_params=pltpu.CompilerParams(collective_id=tag, has_side_effects=True),
    )(values)


def gather_rows(values, axes, parts):
    copies = jnp.broadcast_to(values[None], (parts,) + values.shape)
    return lax.all_to_all(copies, axes, 0, 0, tiled=True).reshape(-1, values.shape[-1])


def scatter_sum(values, axes, parts):
    pieces = lax.all_to_all(values.reshape(parts, -1, values.shape[-1]), axes, 0, 0, tiled=False)
    return pieces.astype(jnp.float32).sum(0)


def body(features, weight, tile_values, tile_row, tile_col, tile_count, cotangent):
    row_count = lax.axis_size("row")
    pair_count = lax.axis_size("colhi")
    core_count = lax.axis_size("core")
    col_count = pair_count * core_count
    node_dev = features.shape[0]
    hidden = features.shape[1]
    tile_size = tile_values.shape[1]
    per_dev = node_dev // tile_size
    row_tiles = node_dev * col_count // tile_size
    col_tiles = node_dev * row_count // tile_size
    core = lax.axis_index("core")
    count = jnp.stack([tile_count.reshape(()), core.astype(jnp.int32)])
    features_block = exchange(features, "row", row_count, True, 0).reshape(-1, hidden)
    panel_rows = jnp.dot(features_block, weight, preferred_element_type=jnp.float32).astype(
        jnp.bfloat16
    )
    swap = [(0, 1), (1, 0)]
    keep, give = tile_products(
        tile_values, tile_col, tile_row, count, panel_rows, row_tiles, True, node_dev
    )
    got = lax.ppermute(give, "core", swap)
    chip_sum = (keep.astype(jnp.float32) + got.astype(jnp.float32)).astype(jnp.bfloat16)
    chip_sum = chip_sum.reshape(pair_count, node_dev, hidden)
    summed = scatter_sum(chip_sum, "colhi", pair_count)
    activated = jax.nn.silu(summed).astype(jnp.bfloat16)
    slope = (cotangent.astype(jnp.float32) * silu_slope(summed)).astype(jnp.bfloat16)
    slope_pairs = gather_rows(slope, "colhi", pair_count)
    slope_full = jnp.concatenate([slope_pairs, lax.ppermute(slope_pairs, "core", swap)], axis=0)
    owner = tile_row // per_dev
    slope_index = (
        (owner % core_count != core).astype(jnp.int32) * (pair_count * per_dev)
        + (owner // core_count) * per_dev
        + tile_row % per_dev
    )
    column_part = tile_products(
        tile_values, slope_index, tile_col, count, slope_full, col_tiles, False
    )
    weight_term = lax.dot_general(
        features_block, column_part, (((0,), (0,)), ((), ())), preferred_element_type=jnp.float32
    )
    term_rows = hidden // row_count
    packed = jnp.concatenate(
        [
            column_part.reshape(row_count, node_dev, hidden),
            weight_term.astype(jnp.bfloat16).reshape(row_count, term_rows, hidden),
        ],
        axis=1,
    )
    reduced = scatter_sum(packed, "row", row_count)
    grad_nodes = reduced[:node_dev].astype(jnp.bfloat16)
    col_terms = gather_rows(reduced[node_dev:], ("colhi", "core"), col_count)
    weight_rows = col_terms.reshape(col_count, term_rows, hidden).sum(0)
    grad_weight = gather_rows(weight_rows, "row", row_count)
    grad_features = lax.dot_general(
        grad_nodes, weight, (((1,), (1,)), ((), ())), preferred_element_type=jnp.float32
    ).astype(jnp.bfloat16)
    return (activated, grad_features, grad_weight)


def solution(mesh):
    rows, cols = mesh.devices.shape
    fine = Mesh(mesh.devices.reshape(rows, cols // 2, 2), ("row", "colhi", "core"))
    col = ("colhi", "core")
    placed = (
        P((*col, "row"), None),
        P(),
        P(("row", *col), None, None),
        P(("row", *col)),
        P(("row", *col)),
        P("row", col),
        P(("row", *col), None),
    )
    return jax.shard_map(
        body,
        mesh=fine,
        in_specs=placed,
        out_specs=(P(("row", *col), None), P((*col, "row"), None), P()),
        check_vma=False,
    )
```

```python
import functools

import jax
import jax.numpy as jnp
from jax import lax
from jax.experimental import pallas as pl
from jax.experimental.pallas import tpu as pltpu
from jax.sharding import Mesh, PartitionSpec as P


GROUP = 64
CHUNK = 256
UNROLL = (64, 8, 1)


def silu_slope(values):
    sigma = jax.nn.sigmoid(values)
    return sigma * (1.0 + values * (1.0 - sigma))


def tile_kernel(count_ref, place_ref, fetch_ref, tiles_ref, src_ref, *refs, forward, block_rows):
    if block_rows:
        keep_ref, give_ref, acc_ref = refs
    else:
        out_ref, acc_ref = refs
    step = pl.program_id(0)
    tile = tiles_ref.shape[1]
    group = tiles_ref.shape[0]
    out_rows = acc_ref.shape[0]

    @pl.when(step == 0)
    def _():
        def zero(k, carry):
            rows = pl.ds(pl.multiple_of(k * CHUNK, CHUNK), CHUNK)
            acc_ref[rows, :] = jnp.zeros((CHUNK, acc_ref.shape[1]), jnp.float32)
            return carry

        lax.fori_loop(0, out_rows // CHUNK, zero, 0)

    base = step * group
    live = jnp.clip(count_ref[0] - base, 0, group)

    def product(slot, j):
        src_rows = pl.ds(pl.multiple_of(fetch_ref[slot] * tile, tile), tile)
        block = tiles_ref[j]
        src = src_ref[src_rows, :]
        if forward:
            return jnp.dot(block, src, preferred_element_type=jnp.float32)
        return lax.dot_general(
            block, src, (((0,), (0,)), ((), ())), preferred_element_type=jnp.float32
        )

    def add(slot, prod):
        dst_rows = pl.ds(pl.multiple_of(place_ref[slot] * tile, tile), tile)
        acc_ref[dst_rows, :] += prod

    def run(start, stop, width):
        def chunk(k, carry):
            j0 = start + k * width
            prods = [product(base + j0 + u, j0 + u) for u in range(width)]
            for u in range(width):
                add(base + j0 + u, prods[u])
            return carry

        chunks = (stop - start) // width
        lax.fori_loop(0, chunks, chunk, 0)
        return start + chunks * width

    done = 0
    for width in UNROLL:
        done = run(done, live, width)

    @pl.when(step == pl.num_programs(0) - 1)
    def _():
        def emit(k, carry):
            rows = pl.ds(pl.multiple_of(k * CHUNK, CHUNK), CHUNK)
            if not block_rows:
                out_ref[rows, :] = acc_ref[rows, :].astype(out_ref.dtype)
                return carry
            values = acc_ref[rows, :].astype(keep_ref.dtype)
            block = k * CHUNK // block_rows
            dst = pl.ds(
                pl.multiple_of((block // 2) * block_rows + k * CHUNK % block_rows, CHUNK), CHUNK
            )

            @pl.when(block % 2 == count_ref[1])
            def _():
                keep_ref[dst, :] = values

            @pl.when(block % 2 != count_ref[1])
            def _():
                give_ref[dst, :] = values

            return carry

        lax.fori_loop(0, out_rows // CHUNK, emit, 0)


def tile_products(tile_values, fetch_index, place_index, count, source, out_tiles, forward, block_rows=0):
    slots, tile, _ = tile_values.shape
    hidden = source.shape[-1]
    src_rows = source.shape[0]
    out_rows = out_tiles * tile
    group = GROUP
    steps = slots // group

    def tiles_map(i, count_ref, place_ref, fetch_ref):
        last = jnp.maximum(count_ref[0] - 1, 0) // group
        return (jnp.minimum(i, last), 0, 0)

    grid_spec = pltpu.PrefetchScalarGridSpec(
        num_scalar_prefetch=3,
        grid=(steps,),
        in_specs=[
            pl.BlockSpec((group, tile, tile), tiles_map),
            pl.BlockSpec((src_rows, hidden), lambda i, *_: (0, 0)),
        ],
        out_specs=[pl.BlockSpec((out_rows // 2, hidden), lambda i, *_: (0, 0))] * 2
        if block_rows
        else pl.BlockSpec((out_rows, hidden), lambda i, *_: (0, 0)),
        scratch_shapes=[pltpu.VMEM((out_rows, hidden), jnp.float32)],
    )
    flops = 2 * slots * tile * tile * hidden
    return pl.pallas_call(
        functools.partial(tile_kernel, forward=forward, block_rows=block_rows),
        grid_spec=grid_spec,
        out_shape=[jax.ShapeDtypeStruct((out_rows // 2, hidden), jnp.bfloat16)] * 2
        if block_rows
        else jax.ShapeDtypeStruct((out_rows, hidden), jnp.bfloat16),
        compiler_params=pltpu.CompilerParams(
            dimension_semantics=("arbitrary",), vmem_limit_bytes=48 * 1024 * 1024
        ),
        cost_estimate=pl.CostEstimate(
            flops=flops,
            bytes_accessed=slots * tile * tile * 2 + src_rows * hidden * 2 + out_rows * hidden * 2,
            transcendentals=0,
        ),
    )(count, place_index, fetch_index, tile_values, source)


def gather_rows(values, axes, parts):
    copies = jnp.broadcast_to(values[None], (parts,) + values.shape)
    return lax.all_to_all(copies, axes, 0, 0, tiled=True).reshape(-1, values.shape[-1])


def scatter_sum(values, axes, parts):
    pieces = lax.all_to_all(values.reshape(parts, -1, values.shape[-1]), axes, 0, 0, tiled=False)
    return pieces.astype(jnp.float32).sum(0)


def body(features, weight, tile_values, tile_row, tile_col, tile_count, cotangent):
    row_count = lax.axis_size("row")
    pair_count = lax.axis_size("colhi")
    core_count = lax.axis_size("core")
    col_count = pair_count * core_count
    node_dev = features.shape[0]
    hidden = features.shape[1]
    tile_size = tile_values.shape[1]
    per_dev = node_dev // tile_size
    row_tiles = node_dev * col_count // tile_size
    col_tiles = node_dev * row_count // tile_size
    core = lax.axis_index("core")
    count = jnp.stack([tile_count.reshape(()), core.astype(jnp.int32)])
    features_block = gather_rows(features, "row", row_count)
    panel_rows = jnp.dot(features_block, weight, preferred_element_type=jnp.float32).astype(
        jnp.bfloat16
    )
    swap = [(0, 1), (1, 0)]
    keep, give = tile_products(
        tile_values, tile_col, tile_row, count, panel_rows, row_tiles, True, node_dev
    )
    got = lax.ppermute(give, "core", swap)
    chip_sum = (keep.astype(jnp.float32) + got.astype(jnp.float32)).astype(jnp.bfloat16)
    chip_sum = chip_sum.reshape(pair_count, node_dev, hidden)
    summed = scatter_sum(chip_sum, "colhi", pair_count)
    activated = jax.nn.silu(summed).astype(jnp.bfloat16)
    slope = (cotangent.astype(jnp.float32) * silu_slope(summed)).astype(jnp.bfloat16)
    slope_pairs = gather_rows(slope, "colhi", pair_count)
    slope_full = jnp.concatenate([slope_pairs, lax.ppermute(slope_pairs, "core", swap)], axis=0)
    owner = tile_row // per_dev
    slope_index = (
        (owner % core_count != core).astype(jnp.int32) * (pair_count * per_dev)
        + (owner // core_count) * per_dev
        + tile_row % per_dev
    )
    column_part = tile_products(
        tile_values, slope_index, tile_col, count, slope_full, col_tiles, False
    )
    weight_term = lax.dot_general(
        features_block, column_part, (((0,), (0,)), ((), ())), preferred_element_type=jnp.float32
    )
    term_rows = hidden // row_count
    packed = jnp.concatenate(
        [
            column_part.reshape(row_count, node_dev, hidden),
            weight_term.astype(jnp.bfloat16).reshape(row_count, term_rows, hidden),
        ],
        axis=1,
    )
    reduced = scatter_sum(packed, "row", row_count)
    grad_nodes = reduced[:node_dev].astype(jnp.bfloat16)
    chip_terms = reduced[node_dev:] + lax.ppermute(reduced[node_dev:], "core", swap)
    col_terms = gather_rows(chip_terms, "colhi", pair_count)
    weight_rows = col_terms.reshape(pair_count, term_rows, hidden).sum(0)
    grad_weight = gather_rows(weight_rows, "row", row_count)
    grad_features = lax.dot_general(
        grad_nodes, weight, (((1,), (1,)), ((), ())), preferred_element_type=jnp.float32
    ).astype(jnp.bfloat16)
    return (activated, grad_features, grad_weight)


def solution(mesh):
    rows, cols = mesh.devices.shape
    fine = Mesh(mesh.devices.reshape(rows, cols // 2, 2), ("row", "colhi", "core"))
    col = ("colhi", "core")
    placed = (
        P((*col, "row"), None),
        P(),
        P(("row", *col), None, None),
        P(("row", *col)),
        P(("row", *col)),
        P("row", col),
        P(("row", *col), None),
    )
    return jax.shard_map(
        body,
        mesh=fine,
        in_specs=placed,
        out_specs=(P(("row", *col), None), P((*col, "row"), None), P()),
        check_vma=False,
    )
```

```python
import functools

import jax
import jax.numpy as jnp
from jax import lax
from jax.experimental import pallas as pl
from jax.experimental.pallas import tpu as pltpu
from jax.sharding import Mesh, PartitionSpec as P


GROUP = 128
CHUNK = 256
UNROLL = (128, 8, 1)


def silu_slope(values):
    sigma = jax.nn.sigmoid(values)
    return sigma * (1.0 + values * (1.0 - sigma))


def tile_kernel(count_ref, place_ref, fetch_ref, tiles_ref, src_ref, *refs, forward, block_rows):
    if block_rows:
        keep_ref, give_ref, acc_ref = refs
    else:
        out_ref, acc_ref = refs
    step = pl.program_id(0)
    tile = tiles_ref.shape[1]
    group = tiles_ref.shape[0]
    out_rows = acc_ref.shape[0]

    @pl.when(step == 0)
    def _():
        def zero(k, carry):
            rows = pl.ds(pl.multiple_of(k * CHUNK, CHUNK), CHUNK)
            acc_ref[rows, :] = jnp.zeros((CHUNK, acc_ref.shape[1]), jnp.float32)
            return carry

        lax.fori_loop(0, out_rows // CHUNK, zero, 0)

    base = step * group
    live = jnp.clip(count_ref[0] - base, 0, group)

    def product(slot, j):
        src_rows = pl.ds(pl.multiple_of(fetch_ref[slot] * tile, tile), tile)
        block = tiles_ref[j]
        src = src_ref[src_rows, :]
        if forward:
            return jnp.dot(block, src, preferred_element_type=jnp.float32)
        return lax.dot_general(
            block, src, (((0,), (0,)), ((), ())), preferred_element_type=jnp.float32
        )

    def add(slot, prod):
        dst_rows = pl.ds(pl.multiple_of(place_ref[slot] * tile, tile), tile)
        acc_ref[dst_rows, :] += prod

    def run(start, stop, width):
        def chunk(k, carry):
            j0 = start + k * width
            prods = [product(base + j0 + u, j0 + u) for u in range(width)]
            for u in range(width):
                add(base + j0 + u, prods[u])
            return carry

        chunks = (stop - start) // width
        lax.fori_loop(0, chunks, chunk, 0)
        return start + chunks * width

    done = 0
    for width in UNROLL:
        done = run(done, live, width)

    @pl.when(step == pl.num_programs(0) - 1)
    def _():
        def emit(k, carry):
            rows = pl.ds(pl.multiple_of(k * CHUNK, CHUNK), CHUNK)
            if not block_rows:
                out_ref[rows, :] = acc_ref[rows, :].astype(out_ref.dtype)
                return carry
            values = acc_ref[rows, :].astype(keep_ref.dtype)
            block = k * CHUNK // block_rows
            dst = pl.ds(
                pl.multiple_of((block // 2) * block_rows + k * CHUNK % block_rows, CHUNK), CHUNK
            )

            @pl.when(block % 2 == count_ref[1])
            def _():
                keep_ref[dst, :] = values

            @pl.when(block % 2 != count_ref[1])
            def _():
                give_ref[dst, :] = values

            return carry

        lax.fori_loop(0, out_rows // CHUNK, emit, 0)


def tile_products(tile_values, fetch_index, place_index, count, source, out_tiles, forward, block_rows=0):
    slots, tile, _ = tile_values.shape
    hidden = source.shape[-1]
    src_rows = source.shape[0]
    out_rows = out_tiles * tile
    group = GROUP
    steps = slots // group

    def tiles_map(i, count_ref, place_ref, fetch_ref):
        last = jnp.maximum(count_ref[0] - 1, 0) // group
        return (jnp.minimum(i, last), 0, 0)

    grid_spec = pltpu.PrefetchScalarGridSpec(
        num_scalar_prefetch=3,
        grid=(steps,),
        in_specs=[
            pl.BlockSpec((group, tile, tile), tiles_map),
            pl.BlockSpec((src_rows, hidden), lambda i, *_: (0, 0)),
        ],
        out_specs=[pl.BlockSpec((out_rows // 2, hidden), lambda i, *_: (0, 0))] * 2
        if block_rows
        else pl.BlockSpec((out_rows, hidden), lambda i, *_: (0, 0)),
        scratch_shapes=[pltpu.VMEM((out_rows, hidden), jnp.float32)],
    )
    flops = 2 * slots * tile * tile * hidden
    return pl.pallas_call(
        functools.partial(tile_kernel, forward=forward, block_rows=block_rows),
        grid_spec=grid_spec,
        out_shape=[jax.ShapeDtypeStruct((out_rows // 2, hidden), jnp.bfloat16)] * 2
        if block_rows
        else jax.ShapeDtypeStruct((out_rows, hidden), jnp.bfloat16),
        compiler_params=pltpu.CompilerParams(
            dimension_semantics=("arbitrary",), vmem_limit_bytes=48 * 1024 * 1024
        ),
        cost_estimate=pl.CostEstimate(
            flops=flops,
            bytes_accessed=slots * tile * tile * 2 + src_rows * hidden * 2 + out_rows * hidden * 2,
            transcendentals=0,
        ),
    )(count, place_index, fetch_index, tile_values, source)


def gather_rows(values, axes, parts):
    copies = jnp.broadcast_to(values[None], (parts,) + values.shape)
    return lax.all_to_all(copies, axes, 0, 0, tiled=True).reshape(-1, values.shape[-1])


def scatter_sum(values, axes, parts):
    pieces = lax.all_to_all(values.reshape(parts, -1, values.shape[-1]), axes, 0, 0, tiled=False)
    return pieces.astype(jnp.float32).sum(0)


def body(features, weight, tile_values, tile_row, tile_col, tile_count, cotangent):
    row_count = lax.axis_size("row")
    pair_count = lax.axis_size("colhi")
    core_count = lax.axis_size("core")
    col_count = pair_count * core_count
    node_dev = features.shape[0]
    hidden = features.shape[1]
    tile_size = tile_values.shape[1]
    per_dev = node_dev // tile_size
    row_tiles = node_dev * col_count // tile_size
    col_tiles = node_dev * row_count // tile_size
    core = lax.axis_index("core")
    count = jnp.stack([tile_count.reshape(()), core.astype(jnp.int32)])
    features_block = gather_rows(features, "row", row_count)
    panel_rows = jnp.dot(features_block, weight, preferred_element_type=jnp.float32).astype(
        jnp.bfloat16
    )
    swap = [(0, 1), (1, 0)]
    keep, give = tile_products(
        tile_values, tile_col, tile_row, count, panel_rows, row_tiles, True, node_dev
    )
    got = lax.ppermute(give, "core", swap)
    chip_sum = (keep.astype(jnp.float32) + got.astype(jnp.float32)).astype(jnp.bfloat16)
    chip_sum = chip_sum.reshape(pair_count, node_dev, hidden)
    summed = scatter_sum(chip_sum, "colhi", pair_count)
    activated = jax.nn.silu(summed).astype(jnp.bfloat16)
    slope = (cotangent.astype(jnp.float32) * silu_slope(summed)).astype(jnp.bfloat16)
    slope_pairs = gather_rows(slope, "colhi", pair_count)
    slope_full = jnp.concatenate([slope_pairs, lax.ppermute(slope_pairs, "core", swap)], axis=0)
    owner = tile_row // per_dev
    slope_index = (
        (owner % core_count != core).astype(jnp.int32) * (pair_count * per_dev)
        + (owner // core_count) * per_dev
        + tile_row % per_dev
    )
    column_part = tile_products(
        tile_values, slope_index, tile_col, count, slope_full, col_tiles, False
    )
    weight_term = lax.dot_general(
        features_block, column_part, (((0,), (0,)), ((), ())), preferred_element_type=jnp.float32
    )
    term_rows = hidden // row_count
    packed = jnp.concatenate(
        [
            column_part.reshape(row_count, node_dev, hidden),
            weight_term.astype(jnp.bfloat16).reshape(row_count, term_rows, hidden),
        ],
        axis=1,
    )
    reduced = scatter_sum(packed, "row", row_count)
    grad_nodes = reduced[:node_dev].astype(jnp.bfloat16)
    chip_terms = reduced[node_dev:] + lax.ppermute(reduced[node_dev:], "core", swap)
    col_terms = gather_rows(chip_terms, "colhi", pair_count)
    weight_rows = col_terms.reshape(pair_count, term_rows, hidden).sum(0)
    grad_weight = gather_rows(weight_rows, "row", row_count)
    grad_features = lax.dot_general(
        grad_nodes, weight, (((1,), (1,)), ((), ())), preferred_element_type=jnp.float32
    ).astype(jnp.bfloat16)
    return (activated, grad_features, grad_weight)


def solution(mesh):
    rows, cols = mesh.devices.shape
    fine = Mesh(mesh.devices.reshape(rows, cols // 2, 2), ("row", "colhi", "core"))
    col = ("colhi", "core")
    placed = (
        P((*col, "row"), None),
        P(),
        P(("row", *col), None, None),
        P(("row", *col)),
        P(("row", *col)),
        P("row", col),
        P(("row", *col), None),
    )
    return jax.shard_map(
        body,
        mesh=fine,
        in_specs=placed,
        out_specs=(P(("row", *col), None), P((*col, "row"), None), P()),
        check_vma=False,
    )
```

```python
import functools

import jax
import jax.numpy as jnp
from jax import lax
from jax.experimental import pallas as pl
from jax.experimental.pallas import tpu as pltpu
from jax.sharding import Mesh, PartitionSpec as P


GROUP = 64
CHUNK = 256
UNROLL = (64, 8, 1)


def silu_slope(values):
    sigma = jax.nn.sigmoid(values)
    return sigma * (1.0 + values * (1.0 - sigma))


def tile_kernel(count_ref, place_ref, fetch_ref, tiles_ref, feed_ref, *refs, forward, block_rows):
    if block_rows:
        weight_ref, keep_ref, give_ref, acc_ref, src_ref = refs
    else:
        out_ref, acc_ref = refs
        src_ref = feed_ref
    step = pl.program_id(0)
    tile = tiles_ref.shape[1]
    group = tiles_ref.shape[0]
    out_rows = acc_ref.shape[0]

    @pl.when(step == 0)
    def _():
        def zero(k, carry):
            rows = pl.ds(pl.multiple_of(k * CHUNK, CHUNK), CHUNK)
            acc_ref[rows, :] = jnp.zeros((CHUNK, acc_ref.shape[1]), jnp.float32)
            return carry

        lax.fori_loop(0, out_rows // CHUNK, zero, 0)

        if block_rows:

            def project(k, carry):
                rows = pl.ds(pl.multiple_of(k * CHUNK, CHUNK), CHUNK)
                src_ref[rows, :] = jnp.dot(
                    feed_ref[rows, :], weight_ref[...], preferred_element_type=jnp.float32
                ).astype(src_ref.dtype)
                return carry

            lax.fori_loop(0, src_ref.shape[0] // CHUNK, project, 0)

    base = step * group
    live = jnp.clip(count_ref[0] - base, 0, group)

    def product(slot, j):
        src_rows = pl.ds(pl.multiple_of(fetch_ref[slot] * tile, tile), tile)
        block = tiles_ref[j]
        src = src_ref[src_rows, :]
        if forward:
            return jnp.dot(block, src, preferred_element_type=jnp.float32)
        return lax.dot_general(
            block, src, (((0,), (0,)), ((), ())), preferred_element_type=jnp.float32
        )

    def add(slot, prod):
        dst_rows = pl.ds(pl.multiple_of(place_ref[slot] * tile, tile), tile)
        acc_ref[dst_rows, :] += prod

    def run(start, stop, width):
        def chunk(k, carry):
            j0 = start + k * width
            prods = [product(base + j0 + u, j0 + u) for u in range(width)]
            for u in range(width):
                add(base + j0 + u, prods[u])
            return carry

        chunks = (stop - start) // width
        lax.fori_loop(0, chunks, chunk, 0)
        return start + chunks * width

    done = 0
    for width in UNROLL:
        done = run(done, live, width)

    @pl.when(step == pl.num_programs(0) - 1)
    def _():
        def emit(k, carry):
            rows = pl.ds(pl.multiple_of(k * CHUNK, CHUNK), CHUNK)
            if not block_rows:
                out_ref[rows, :] = acc_ref[rows, :].astype(out_ref.dtype)
                return carry
            values = acc_ref[rows, :].astype(keep_ref.dtype)
            block = k * CHUNK // block_rows
            dst = pl.ds(
                pl.multiple_of((block // 2) * block_rows + k * CHUNK % block_rows, CHUNK), CHUNK
            )

            @pl.when(block % 2 == count_ref[1])
            def _():
                keep_ref[dst, :] = values

            @pl.when(block % 2 != count_ref[1])
            def _():
                give_ref[dst, :] = values

            return carry

        lax.fori_loop(0, out_rows // CHUNK, emit, 0)


def tile_products(
    tile_values, fetch_index, place_index, count, source, out_tiles, forward, block_rows=0, weight=None
):
    slots, tile, _ = tile_values.shape
    hidden = source.shape[-1]
    src_rows = source.shape[0]
    out_rows = out_tiles * tile
    group = GROUP
    steps = slots // group

    def tiles_map(i, count_ref, place_ref, fetch_ref):
        last = jnp.maximum(count_ref[0] - 1, 0) // group
        return (jnp.minimum(i, last), 0, 0)

    grid_spec = pltpu.PrefetchScalarGridSpec(
        num_scalar_prefetch=3,
        grid=(steps,),
        in_specs=[
            pl.BlockSpec((group, tile, tile), tiles_map),
            pl.BlockSpec((src_rows, hidden), lambda i, *_: (0, 0)),
        ]
        + ([pl.BlockSpec((hidden, hidden), lambda i, *_: (0, 0))] if block_rows else []),
        out_specs=[pl.BlockSpec((out_rows // 2, hidden), lambda i, *_: (0, 0))] * 2
        if block_rows
        else pl.BlockSpec((out_rows, hidden), lambda i, *_: (0, 0)),
        scratch_shapes=[pltpu.VMEM((out_rows, hidden), jnp.float32)]
        + ([pltpu.VMEM((src_rows, hidden), jnp.bfloat16)] if block_rows else []),
    )
    flops = 2 * slots * tile * tile * hidden
    return pl.pallas_call(
        functools.partial(tile_kernel, forward=forward, block_rows=block_rows),
        grid_spec=grid_spec,
        out_shape=[jax.ShapeDtypeStruct((out_rows // 2, hidden), jnp.bfloat16)] * 2
        if block_rows
        else jax.ShapeDtypeStruct((out_rows, hidden), jnp.bfloat16),
        compiler_params=pltpu.CompilerParams(
            dimension_semantics=("arbitrary",), vmem_limit_bytes=48 * 1024 * 1024
        ),
        cost_estimate=pl.CostEstimate(
            flops=flops,
            bytes_accessed=slots * tile * tile * 2 + src_rows * hidden * 2 + out_rows * hidden * 2,
            transcendentals=0,
        ),
    )(count, place_index, fetch_index, tile_values, source, *([weight] if block_rows else []))


def gather_rows(values, axes, parts):
    copies = jnp.broadcast_to(values[None], (parts,) + values.shape)
    return lax.all_to_all(copies, axes, 0, 0, tiled=True).reshape(-1, values.shape[-1])


def scatter_sum(values, axes, parts):
    pieces = lax.all_to_all(values.reshape(parts, -1, values.shape[-1]), axes, 0, 0, tiled=False)
    return pieces.astype(jnp.float32).sum(0)


def body(features, weight, tile_values, tile_row, tile_col, tile_count, cotangent):
    row_count = lax.axis_size("row")
    pair_count = lax.axis_size("colhi")
    core_count = lax.axis_size("core")
    col_count = pair_count * core_count
    node_dev = features.shape[0]
    hidden = features.shape[1]
    tile_size = tile_values.shape[1]
    per_dev = node_dev // tile_size
    row_tiles = node_dev * col_count // tile_size
    col_tiles = node_dev * row_count // tile_size
    core = lax.axis_index("core")
    count = jnp.stack([tile_count.reshape(()), core.astype(jnp.int32)])
    features_block = gather_rows(features, "row", row_count)
    swap = [(0, 1), (1, 0)]
    keep, give = tile_products(
        tile_values, tile_col, tile_row, count, features_block, row_tiles, True, node_dev, weight
    )
    got = lax.ppermute(give, "core", swap)
    chip_sum = (keep.astype(jnp.float32) + got.astype(jnp.float32)).astype(jnp.bfloat16)
    chip_sum = chip_sum.reshape(pair_count, node_dev, hidden)
    summed = scatter_sum(chip_sum, "colhi", pair_count)
    activated = jax.nn.silu(summed).astype(jnp.bfloat16)
    slope = (cotangent.astype(jnp.float32) * silu_slope(summed)).astype(jnp.bfloat16)
    slope_pairs = gather_rows(slope, "colhi", pair_count)
    slope_full = jnp.concatenate([slope_pairs, lax.ppermute(slope_pairs, "core", swap)], axis=0)
    owner = tile_row // per_dev
    slope_index = (
        (owner % core_count != core).astype(jnp.int32) * (pair_count * per_dev)
        + (owner // core_count) * per_dev
        + tile_row % per_dev
    )
    column_part = tile_products(
        tile_values, slope_index, tile_col, count, slope_full, col_tiles, False
    )
    weight_term = lax.dot_general(
        features_block, column_part, (((0,), (0,)), ((), ())), preferred_element_type=jnp.float32
    )
    term_rows = hidden // row_count
    packed = jnp.concatenate(
        [
            column_part.reshape(row_count, node_dev, hidden),
            weight_term.astype(jnp.bfloat16).reshape(row_count, term_rows, hidden),
        ],
        axis=1,
    )
    reduced = scatter_sum(packed, "row", row_count)
    grad_nodes = reduced[:node_dev].astype(jnp.bfloat16)
    chip_terms = reduced[node_dev:] + lax.ppermute(reduced[node_dev:], "core", swap)
    col_terms = gather_rows(chip_terms, "colhi", pair_count)
    weight_rows = col_terms.reshape(pair_count, term_rows, hidden).sum(0)
    grad_weight = gather_rows(weight_rows, "row", row_count)
    grad_features = lax.dot_general(
        grad_nodes, weight, (((1,), (1,)), ((), ())), preferred_element_type=jnp.float32
    ).astype(jnp.bfloat16)
    return (activated, grad_features, grad_weight)


def solution(mesh):
    rows, cols = mesh.devices.shape
    fine = Mesh(mesh.devices.reshape(rows, cols // 2, 2), ("row", "colhi", "core"))
    col = ("colhi", "core")
    placed = (
        P((*col, "row"), None),
        P(),
        P(("row", *col), None, None),
        P(("row", *col)),
        P(("row", *col)),
        P("row", col),
        P(("row", *col), None),
    )
    return jax.shard_map(
        body,
        mesh=fine,
        in_specs=placed,
        out_specs=(P(("row", *col), None), P((*col, "row"), None), P()),
        check_vma=False,
    )
```

```python
import functools

import jax
import jax.numpy as jnp
from jax import lax
from jax.experimental import pallas as pl
from jax.experimental.pallas import tpu as pltpu
from jax.sharding import Mesh, PartitionSpec as P


GROUP = 64
CHUNK = 512
UNROLL = (64, 8, 1)


def silu_slope(values):
    sigma = jax.nn.sigmoid(values)
    return sigma * (1.0 + values * (1.0 - sigma))


def tile_kernel(count_ref, place_ref, fetch_ref, tiles_ref, src_ref, *refs, forward, block_rows):
    if block_rows:
        keep_ref, give_ref, acc_ref = refs
    else:
        out_ref, acc_ref = refs
    step = pl.program_id(0)
    tile = tiles_ref.shape[1]
    group = tiles_ref.shape[0]
    out_rows = acc_ref.shape[0]

    @pl.when(step == 0)
    def _():
        def zero(k, carry):
            rows = pl.ds(pl.multiple_of(k * CHUNK, CHUNK), CHUNK)
            acc_ref[rows, :] = jnp.zeros((CHUNK, acc_ref.shape[1]), jnp.float32)
            return carry

        lax.fori_loop(0, out_rows // CHUNK, zero, 0)

    base = step * group
    live = jnp.clip(count_ref[0] - base, 0, group)

    def product(slot, j):
        src_rows = pl.ds(pl.multiple_of(fetch_ref[slot] * tile, tile), tile)
        block = tiles_ref[j]
        src = src_ref[src_rows, :]
        if forward:
            return jnp.dot(block, src, preferred_element_type=jnp.float32)
        return lax.dot_general(
            block, src, (((0,), (0,)), ((), ())), preferred_element_type=jnp.float32
        )

    def add(slot, prod):
        dst_rows = pl.ds(pl.multiple_of(place_ref[slot] * tile, tile), tile)
        acc_ref[dst_rows, :] += prod

    def run(start, stop, width):
        def chunk(k, carry):
            j0 = start + k * width
            prods = [product(base + j0 + u, j0 + u) for u in range(width)]
            for u in range(width):
                add(base + j0 + u, prods[u])
            return carry

        chunks = (stop - start) // width
        lax.fori_loop(0, chunks, chunk, 0)
        return start + chunks * width

    done = 0
    for width in UNROLL:
        done = run(done, live, width)

    @pl.when(step == pl.num_programs(0) - 1)
    def _():
        def emit(k, carry):
            rows = pl.ds(pl.multiple_of(k * CHUNK, CHUNK), CHUNK)
            if not block_rows:
                out_ref[rows, :] = acc_ref[rows, :].astype(out_ref.dtype)
                return carry
            values = acc_ref[rows, :].astype(keep_ref.dtype)
            block = k * CHUNK // block_rows
            dst = pl.ds(
                pl.multiple_of((block // 2) * block_rows + k * CHUNK % block_rows, CHUNK), CHUNK
            )

            @pl.when(block % 2 == count_ref[1])
            def _():
                keep_ref[dst, :] = values

            @pl.when(block % 2 != count_ref[1])
            def _():
                give_ref[dst, :] = values

            return carry

        lax.fori_loop(0, out_rows // CHUNK, emit, 0)


def tile_products(tile_values, fetch_index, place_index, count, source, out_tiles, forward, block_rows=0):
    slots, tile, _ = tile_values.shape
    hidden = source.shape[-1]
    src_rows = source.shape[0]
    out_rows = out_tiles * tile
    group = GROUP
    steps = slots // group

    def tiles_map(i, count_ref, place_ref, fetch_ref):
        last = jnp.maximum(count_ref[0] - 1, 0) // group
        return (jnp.minimum(i, last), 0, 0)

    grid_spec = pltpu.PrefetchScalarGridSpec(
        num_scalar_prefetch=3,
        grid=(steps,),
        in_specs=[
            pl.BlockSpec((group, tile, tile), tiles_map),
            pl.BlockSpec((src_rows, hidden), lambda i, *_: (0, 0)),
        ],
        out_specs=[pl.BlockSpec((out_rows // 2, hidden), lambda i, *_: (0, 0))] * 2
        if block_rows
        else pl.BlockSpec((out_rows, hidden), lambda i, *_: (0, 0)),
        scratch_shapes=[pltpu.VMEM((out_rows, hidden), jnp.float32)],
    )
    flops = 2 * slots * tile * tile * hidden
    return pl.pallas_call(
        functools.partial(tile_kernel, forward=forward, block_rows=block_rows),
        grid_spec=grid_spec,
        out_shape=[jax.ShapeDtypeStruct((out_rows // 2, hidden), jnp.bfloat16)] * 2
        if block_rows
        else jax.ShapeDtypeStruct((out_rows, hidden), jnp.bfloat16),
        compiler_params=pltpu.CompilerParams(
            dimension_semantics=("arbitrary",), vmem_limit_bytes=48 * 1024 * 1024
        ),
        cost_estimate=pl.CostEstimate(
            flops=flops,
            bytes_accessed=slots * tile * tile * 2 + src_rows * hidden * 2 + out_rows * hidden * 2,
            transcendentals=0,
        ),
    )(count, place_index, fetch_index, tile_values, source)


def gather_rows(values, axes, parts):
    copies = jnp.broadcast_to(values[None], (parts,) + values.shape)
    return lax.all_to_all(copies, axes, 0, 0, tiled=True).reshape(-1, values.shape[-1])


def scatter_sum(values, axes, parts):
    pieces = lax.all_to_all(values.reshape(parts, -1, values.shape[-1]), axes, 0, 0, tiled=False)
    return pieces.astype(jnp.float32).sum(0)


def body(features, weight, tile_values, tile_row, tile_col, tile_count, cotangent):
    row_count = lax.axis_size("row")
    pair_count = lax.axis_size("colhi")
    core_count = lax.axis_size("core")
    col_count = pair_count * core_count
    node_dev = features.shape[0]
    hidden = features.shape[1]
    tile_size = tile_values.shape[1]
    per_dev = node_dev // tile_size
    row_tiles = node_dev * col_count // tile_size
    col_tiles = node_dev * row_count // tile_size
    core = lax.axis_index("core")
    count = jnp.stack([tile_count.reshape(()), core.astype(jnp.int32)])
    features_block = gather_rows(features, "row", row_count)
    panel_rows = jnp.dot(features_block, weight, preferred_element_type=jnp.float32).astype(
        jnp.bfloat16
    )
    swap = [(0, 1), (1, 0)]
    keep, give = tile_products(
        tile_values, tile_col, tile_row, count, panel_rows, row_tiles, True, node_dev
    )
    got = lax.ppermute(give, "core", swap)
    chip_sum = (keep.astype(jnp.float32) + got.astype(jnp.float32)).astype(jnp.bfloat16)
    chip_sum = chip_sum.reshape(pair_count, node_dev, hidden)
    summed = scatter_sum(chip_sum, "colhi", pair_count)
    activated = jax.nn.silu(summed).astype(jnp.bfloat16)
    slope = (cotangent.astype(jnp.float32) * silu_slope(summed)).astype(jnp.bfloat16)
    slope_pairs = gather_rows(slope, "colhi", pair_count)
    slope_full = jnp.concatenate([slope_pairs, lax.ppermute(slope_pairs, "core", swap)], axis=0)
    owner = tile_row // per_dev
    slope_index = (
        (owner % core_count != core).astype(jnp.int32) * (pair_count * per_dev)
        + (owner // core_count) * per_dev
        + tile_row % per_dev
    )
    column_part = tile_products(
        tile_values, slope_index, tile_col, count, slope_full, col_tiles, False
    )
    weight_term = lax.dot_general(
        features_block, column_part, (((0,), (0,)), ((), ())), preferred_element_type=jnp.float32
    )
    term_rows = hidden // row_count
    packed = jnp.concatenate(
        [
            column_part.reshape(row_count, node_dev, hidden),
            weight_term.astype(jnp.bfloat16).reshape(row_count, term_rows, hidden),
        ],
        axis=1,
    )
    reduced = scatter_sum(packed, "row", row_count)
    grad_nodes = reduced[:node_dev].astype(jnp.bfloat16)
    chip_terms = reduced[node_dev:] + lax.ppermute(reduced[node_dev:], "core", swap)
    col_terms = gather_rows(chip_terms, "colhi", pair_count)
    weight_rows = col_terms.reshape(pair_count, term_rows, hidden).sum(0)
    grad_weight = gather_rows(weight_rows, "row", row_count)
    grad_features = lax.dot_general(
        grad_nodes, weight, (((1,), (1,)), ((), ())), preferred_element_type=jnp.float32
    ).astype(jnp.bfloat16)
    return (activated, grad_features, grad_weight)


def solution(mesh):
    rows, cols = mesh.devices.shape
    fine = Mesh(mesh.devices.reshape(rows, cols // 2, 2), ("row", "colhi", "core"))
    col = ("colhi", "core")
    placed = (
        P((*col, "row"), None),
        P(),
        P(("row", *col), None, None),
        P(("row", *col)),
        P(("row", *col)),
        P("row", col),
        P(("row", *col), None),
    )
    return jax.shard_map(
        body,
        mesh=fine,
        in_specs=placed,
        out_specs=(P(("row", *col), None), P((*col, "row"), None), P()),
        check_vma=False,
    )
```
